32 devices in a mesh: expert: 16 (over z, y, core), half: 2 (over x).
Axes of the slice: x: 2, y: 2, z: 4, core: 2. Of those that a mesh axis runs over, the one named last changes fastest.
Arguments:
- tokens: bfloat16 [256, 2048], P('expert', 'half'), may hold values from -6 to 6
- upstream: bfloat16 [256, 2048], P('expert', 'half'), may hold values from -6 to 6
- expert_ids: int32 [256, 8], P('expert'), may hold values from 0 to 15, all different within a row; in each aligned block of 16 rows (0 to 15, 16 to 31, ...) at most 16 rows name the same one
- gate_probs: float32 [256, 8], P('expert'), may hold values from 0.01 to 1
- pad_mask: int32 [256], P('expert'), may hold values 0 or 1
- gate_weight: bfloat16 [16, 2048, 1536], P('expert', None, 'half'), may hold values from -0.125 to 0.125
- up_weight: bfloat16 [16, 2048, 1536], P('expert', None, 'half'), may hold values from -0.125 to 0.125
- down_weight: bfloat16 [16, 1536, 2048], P('expert', 'half'), may hold values from -0.15625 to 0.15625
Outputs:
- layer_out: bfloat16 [256, 2048], P('expert', 'half')
- grad_tokens: bfloat16 [256, 2048], P('expert', 'half')
The draws below stay inside these ranges and needn't reach their ends.
Inputs may be any that keep to these rules, and one draw needn't show every extreme that they name: `expert_ids`: each row names 8 different experts. In the rows of one device (aligned blocks of 16 rows) no expert is named more than 16 times, a bound that some block reaches.
All inputs are finite; a program needn't handle non-finite values. No bound on the sum of `pad_mask` on one device may be relied on, other than what follows from the above.
Results may differ from the reference program's by a relative error of at most 0.025.
Values may be sent and summed in bfloat16 or wider, within the bound.
A program may use at most 64 MiB of HBM per device.

```python
import math
import jax
import jax.numpy as jnp
import numpy as np
from jax import lax

D = 2048
HID = 1536
TOPK = 8
TOK_DEV = 16
EXPERTS = 16
CAP = 16
TOKENS = 256
N_EXPERT = 16
N_HALF = 2


def touch_ends(entries, rng, least, high):
    longest = entries.shape.index(max(entries.shape))
    spots = []
    for shift in (0, 1):
        where = [jax.random.randint(jax.random.fold_in(rng, axis), (), 0, length) for axis, length in enumerate(entries.shape)]
        where[longest] = (where[longest] + shift) % entries.shape[longest]
        spots.append(tuple(where))
    return entries.at[spots[0]].set(least).at[spots[1]].set(high)


def shard_levels(rng, shape, split, least, high):
    level, own = 1.0, jax.random.fold_in(rng, 6)
    for dim, shards_of in split:
        heights = jnp.exp(jax.random.uniform(jax.random.fold_in(own, dim), (shards_of,), jnp.float32, least / len(split), high / len(split)))
        level = level * jnp.repeat(heights, shape[dim] // shards_of).reshape([-1 if axis == dim else 1 for axis in range(len(shape))])
    return level


def shared_out(key, own, number, rows, count, top, most, slope):
    sequence = jax.random.permutation(key, count)
    heavy_load, usual = portions_of(count, rows * top, most, slope, True), portions_of(count, rows * top, most, slope, False)
    places = jnp.arange(count)

    def named(lengths, offset_by):
        used = int((lengths > 0).sum())
        fixed = max(1, used // 4)
        moved = fixed + (places - fixed + offset_by * (used - fixed)) % max(1, count - fixed)
        return jnp.zeros((count,), jnp.int32).at[sequence[jnp.where(places < fixed, places, moved)]].set(jnp.asarray(lengths, jnp.int32))

    lengths = jnp.where(number % 4 == 0, named(heavy_load, number // 4), named(usual, number - number // 4 - 1))
    mixed = jax.random.permutation(jax.random.fold_in(own, 3), count)
    source_of, sink = mixed[0:count // 2 * 2:2], mixed[1:count // 2 * 2:2]
    margin = jnp.minimum(lengths[source_of] - 1, most - lengths[sink]) // 2
    margin = jnp.where((source_of == sequence[0]) | (sink == sequence[0]) | (lengths[sink] == 0), 0, jnp.maximum(margin, 0))
    moved = jax.random.randint(jax.random.fold_in(own, 4), (count // 2,), 0, 1 << 20) % (margin + 1)
    lengths = lengths.at[source_of].add(-moved).at[sink].add(moved)
    items = jnp.searchsorted(jnp.cumsum(lengths), jnp.arange(rows * top), side="right").astype(jnp.int32)
    listing = items.reshape(top, rows).T
    listing = listing[jax.random.permutation(jax.random.fold_in(own, 1), rows)]
    offset_by = jax.random.randint(jax.random.fold_in(own, 2), (rows, 1), 0, top)
    return jnp.take_along_axis(listing, (jnp.arange(top)[None, :] + offset_by) % top, axis=1)


def portions_of(count, total, reach, skew, full):
    weights = [(1 << 20) // math.isqrt(rank ** skew) + 1 for rank in range(1, count + 1)]
    largest = reach if full else min(reach, max(-(-total // count), total * weights[0] // sum(weights)))
    least = 1 if total - largest >= count - 1 else 0
    counts, surplus = [largest] + [least] * (count - 1), total - largest - least * (count - 1)
    while surplus > 0:
        movable = [i for i in range(1, count) if counts[i] < largest] or [i for i in range(1, count) if counts[i] < reach]
        pool, budget = sum([weights[i] for i in movable]), surplus
        for i in movable:
            extra = min(reach - counts[i], max(1, budget * weights[i] // pool), surplus)
            counts[i] = counts[i] + extra
            surplus = surplus - extra
    return np.array(counts)


def noise(key, extent, scale, bound, shards=(), kind=jnp.bfloat16):
    drawn = jax.random.normal(key, extent, jnp.float32) * scale
    if len(shards) > 0:
        drawn = shard_levels(key, extent, shards, -0.22, 0.18) * drawn
    return jnp.clip(drawn, min=-bound, max=bound).astype(kind)


def setup_inputs(seed: int = 0) -> dict:
    key_of = jax.random.split(jax.random.key(seed), 9)
    tokens = noise(key_of[0], (TOKENS, D), 1.0, 6.0, ((0, 16), (1, 2)))
    upstream = noise(key_of[1], (TOKENS, D), 1.0, 6.0, ((0, 16), (1, 2)))
    expert_ids_keys = jax.random.split(jax.random.fold_in(key_of[2], 1), TOKENS // TOK_DEV)
    expert_ids_turns = jax.random.permutation(jax.random.fold_in(key_of[2], 3), TOKENS // TOK_DEV)
    expert_ids = jax.vmap(lambda own, number: shared_out(jax.random.fold_in(key_of[2], 2), own, number, TOK_DEV, EXPERTS, TOPK, CAP, 2))(expert_ids_keys, expert_ids_turns).reshape((TOKENS, TOPK))
    gate_probs = jnp.clip(jnp.exp(math.log(1.0) - 4.6051702 * jax.random.uniform(key_of[3], (TOKENS, TOPK), jnp.float32) ** shard_levels(key_of[3], (TOKENS, TOPK), ((0, 16),), -0.2, 0.2)), 0.01, 1.0)
    pad_mask = touch_ends((jax.random.randint(key_of[4], (TOKENS,), 0, 8) < 7).astype(jnp.int32), jax.random.fold_in(key_of[4], 1), 0, 1)
    gate_weight = noise(key_of[5], (EXPERTS, D, HID), D ** -0.5, 0.125, ((0, 16), (2, 2)))
    up_weight = noise(key_of[6], (EXPERTS, D, HID), D ** -0.5, 0.125, ((0, 16), (2, 2)))
    down_weight = noise(key_of[7], (EXPERTS, HID, D), HID ** -0.5, 0.15625, ((0, 16), (1, 2)))
    return {"tokens": tokens, "upstream": upstream, "expert_ids": expert_ids, "gate_probs": gate_probs, "pad_mask": pad_mask, "gate_weight": gate_weight, "up_weight": up_weight, "down_weight": down_weight}


orth_weight = 0.25

def slot_numbers(expert_ids):
    blocks = expert_ids.reshape(N_EXPERT, TOK_DEV * TOPK)
    onehot = (blocks[:, :, None] == jnp.arange(EXPERTS, dtype=jnp.int32)[None, None, :]).astype(jnp.int32)
    before = jnp.cumsum(onehot, axis=1) - onehot
    slot_index = lax.optimization_barrier(jnp.sum(before * onehot, axis=2))
    return slot_index.reshape(TOKENS * TOPK).astype(jnp.int32)

def rounded(value):
    return lax.optimization_barrier(value.astype(jnp.bfloat16)).astype(jnp.float32)

def reference(tokens, upstream, expert_ids, gate_probs, pad_mask, gate_weight, up_weight, down_weight):
    piece_width = HID // N_HALF
    slot_index = slot_numbers(expert_ids)
    flat_ids = expert_ids.reshape(TOKENS * TOPK).astype(jnp.int32)
    item_index = jnp.arange(TOKENS * TOPK, dtype=jnp.int32)
    source = item_index // (TOK_DEV * TOPK)
    table = jnp.full((EXPERTS, N_EXPERT * CAP), -1, jnp.int32)
    table = table.at[flat_ids, source * CAP + slot_index].set(item_index)

    def expert_inputs(row_ids):
        valid = row_ids >= 0
        safe = jnp.where(valid, row_ids, 0)
        rows_in = jnp.where(valid[:, None], tokens[safe // TOPK], jnp.zeros((), jnp.bfloat16))
        return (valid, safe, rows_in)

    def forward(carry, packed):
        row_ids, weight_gate, weight_up, weight_down = packed
        valid, safe, rows_in = expert_inputs(row_ids)
        gate_val = jnp.dot(rows_in, weight_gate, preferred_element_type=jnp.float32)
        up_val = jnp.dot(rows_in, weight_up, preferred_element_type=jnp.float32)
        hidden_act = (jax.nn.silu(gate_val) * up_val).astype(jnp.bfloat16)
        total = jnp.zeros((N_EXPERT * CAP, D), jnp.float32)
        for piece in range(N_HALF):
            lower = piece * piece_width
            term = jnp.dot(hidden_act[:, lower:lower + piece_width], weight_down[lower:lower + piece_width], preferred_element_type=jnp.float32)
            total = total + rounded(term)
        out_rows = total.astype(jnp.bfloat16)
        target = jnp.where(valid, safe, TOKENS * TOPK)
        carry = carry.at[target].set(out_rows, mode='drop')
        return (carry, None)
    outputs, _ = lax.scan(forward, jnp.zeros((TOKENS * TOPK, D), jnp.bfloat16), (table, gate_weight, up_weight, down_weight))
    out_float = outputs.reshape(TOKENS, TOPK, D).astype(jnp.float32)
    shares = gate_probs / lax.optimization_barrier(jnp.sum(gate_probs, axis=1, keepdims=True))
    layer_out = lax.optimization_barrier(jnp.sum(shares[:, :, None] * out_float, axis=1)).astype(jnp.bfloat16)
    gram = jnp.einsum('tjd,tkd->tjk', out_float, out_float) / jnp.sqrt(jnp.float32(D))
    off_diag = 1.0 - jnp.eye(TOPK, dtype=jnp.float32)
    coeffs = orth_weight * gram * off_diag
    grad_out = pad_mask.astype(jnp.float32)[:, None, None] * (shares[:, :, None] * upstream.astype(jnp.float32)[:, None, :] + jnp.einsum('tjk,tkd->tjd', coeffs, out_float))
    grad_items = grad_out.astype(jnp.bfloat16).reshape(TOKENS * TOPK, D)

    def backward(carry, packed):
        row_ids, weight_gate, weight_up, weight_down = packed
        valid, safe, rows_in = expert_inputs(row_ids)
        gate_val = jnp.dot(rows_in, weight_gate, preferred_element_type=jnp.float32)
        up_val = jnp.dot(rows_in, weight_up, preferred_element_type=jnp.float32)
        grad_rows = jnp.where(valid[:, None], grad_items[safe], jnp.zeros((), jnp.bfloat16))
        grad_act = jnp.dot(grad_rows, weight_down.T, preferred_element_type=jnp.float32)
        sigma = jax.nn.sigmoid(gate_val)
        grad_gate = (grad_act * up_val * sigma * (1.0 + gate_val * (1.0 - sigma))).astype(jnp.bfloat16)
        grad_up = (grad_act * gate_val * sigma).astype(jnp.bfloat16)
        total = jnp.zeros((N_EXPERT * CAP, D), jnp.float32)
        for piece in range(N_HALF):
            lower = piece * piece_width
            term = jnp.dot(grad_gate[:, lower:lower + piece_width], weight_gate[:, lower:lower + piece_width].T, preferred_element_type=jnp.float32)
            term = term + jnp.dot(grad_up[:, lower:lower + piece_width], weight_up[:, lower:lower + piece_width].T, preferred_element_type=jnp.float32)
            total = total + rounded(term)
        grad_in_rows = total.astype(jnp.bfloat16).astype(jnp.float32)
        target = jnp.where(valid, safe // TOPK, TOKENS)
        carry = carry.at[target].add(grad_in_rows, mode='drop')
        return (carry, None)
    grad_sum, _ = lax.scan(backward, jnp.zeros((TOKENS, D), jnp.float32), (table, gate_weight, up_weight, down_weight))
    return (layer_out, grad_sum.astype(jnp.bfloat16))
```

```python
import functools
import math

import jax
import jax.numpy as jnp
from jax import lax
from jax.experimental import pallas as pl
from jax.experimental.pallas import tpu as pltpu
from jax.sharding import PartitionSpec as P

orth_weight = 0.25


def assign_slots(expert_ids, experts, capacity):
    tok_count, top_count = expert_ids.shape
    flat_ids = expert_ids.reshape(tok_count * top_count)
    onehot = (flat_ids[:, None] == jnp.arange(experts, dtype=jnp.int32)[None, :]).astype(jnp.int32)
    before = jnp.cumsum(onehot, axis=0) - onehot
    slot_index = jnp.sum(before * onehot, axis=1)
    return flat_ids * capacity + slot_index


def placement_matrix(slot_dest, slots_total):
    row_index = jnp.arange(slots_total, dtype=jnp.int32)
    return (row_index[:, None] == slot_dest[None, :]).astype(jnp.bfloat16)


def to_experts(place, items):
    whole = lax.all_gather(items, "half", axis=1, tiled=True)
    buckets = jnp.dot(place, whole, preferred_element_type=jnp.float32).astype(jnp.bfloat16)
    return lax.all_to_all(buckets, "expert", split_axis=0, concat_axis=0, tiled=True)


def to_homes(partial_value):
    summed = lax.psum_scatter(
        partial_value.astype(jnp.bfloat16), "half", scatter_dimension=1, tiled=True
    )
    return lax.all_to_all(summed, "expert", split_axis=0, concat_axis=0, tiled=True)


def block_of(width):
    return next((b for b in (256, 128) if width % b == 0), width)


def tiles(width, body):
    size = block_of(width)

    def step(j, carry):
        body(pl.ds(pl.multiple_of(j * size, size), size), size)
        return carry

    lax.fori_loop(0, width // size, step, 0)


def dot(a, b):
    return jnp.dot(a, b, preferred_element_type=jnp.float32)


def dot_t(a, b):
    return lax.dot_general(a, b, (((1,), (1,)), ((), ())), preferred_element_type=jnp.float32)


def fused_kernel(
    n, halves,
    tokens_ref, up_ref, ids_ref, probs_ref, pad_ref, wg_hbm, wu_hbm, wd_hbm,
    layer_ref, gtok_ref,
    tok_buf, wg, wu, wd, gate_v, up_v, hid, gg, gu,
    osend, xrecv, xs, gram_s, gsend, grows, psend, prec, rsend, fin,
    w_sem, tok_ss, tok_rs, out_ss, out_rs, gram_ss, gram_rs, grad_ss, grad_rs,
    pair_ss, pair_rs, fin_ss, fin_rs,
):
    e = lax.axis_index("expert")
    h = lax.axis_index("half")
    tok, width = tokens_ref.shape
    hidden = wg.shape[1]
    rows = n * tok
    chips = n // 2
    parity = lax.rem(e, 2)
    chip = lax.div(e, 2)
    sibling = e + 1 - 2 * parity
    full = halves * width

    def remote(src, dst, ssem, rsem, pe, ph):
        return pltpu.make_async_remote_copy(
            src_ref=src, dst_ref=dst, send_sem=ssem, recv_sem=rsem,
            device_id=(pe, ph), device_id_type=pl.DeviceIdType.MESH,
        )

    def wrap(a, d, size):
        return lax.rem(a + d, size)

    loads = [
        pltpu.make_async_copy(src.at[0], dst, w_sem.at[i])
        for i, (src, dst) in enumerate(((wg_hbm, wg), (wu_hbm, wu), (wd_hbm, wd)))
    ]
    for c in loads:
        c.start()

    everyone = [(de, dh) for de in range(n) for dh in range(halves) if de or dh]
    barrier = pltpu.get_barrier_semaphore()
    for de, dh in everyone:
        pl.semaphore_signal(
            barrier, inc=1, device_id=(wrap(e, de, n), wrap(h, dh, halves)),
            device_id_type=pl.DeviceIdType.MESH,
        )
    pl.semaphore_wait(barrier, len(everyone))

    sends = []
    far = [(dm, dh) for dm in range(chips) for dh in range(halves) if dm or dh]
    k = 0
    for dm, dh in far:
        c = remote(
            tokens_ref, tok_buf.at[h, e], tok_ss.at[k], tok_rs.at[h, e],
            2 * wrap(chip, dm, chips) + parity, wrap(h, dh, halves),
        )
        c.start()
        sends.append(c)
        k += 1
    c = remote(tokens_ref, tok_buf.at[h, e], tok_ss.at[k], tok_rs.at[h, e], sibling, h)
    c.start()
    sends.append(c)
    k += 1
    tok_buf[h, e] = tokens_ref[...]
    for dm, dh in far:
        pe = 2 * wrap(chip, chips - dm, chips) + parity
        ph = wrap(h, halves - dh, halves)
        slot = tok_buf.at[ph, pe]
        c = remote(slot, slot, tok_ss.at[k], tok_rs.at[ph, pe], sibling, h)
        c.wait_recv()
        c.start()
        sends.append(c)
        k += 1
    slot = tok_buf.at[h, sibling]
    remote(slot, slot, tok_ss.at[0], tok_rs.at[h, sibling], sibling, h).wait_recv()
    for dm, dh in far:
        pe = 2 * wrap(chip, chips - dm, chips) + 1 - parity
        ph = wrap(h, halves - dh, halves)
        slot = tok_buf.at[ph, pe]
        remote(slot, slot, tok_ss.at[0], tok_rs.at[ph, pe], sibling, h).wait_recv()

    loads[0].wait()
    loads[1].wait()

    def hidden_step(cols, size):
        gate = jnp.zeros((rows, size), jnp.float32)
        up = jnp.zeros((rows, size), jnp.float32)
        for i in range(halves):
            x = tok_buf[i].reshape(rows, width)
            gate = gate + dot(x, wg[i * width:(i + 1) * width, cols])
            up = up + dot(x, wu[i * width:(i + 1) * width, cols])
        gate_v[:, cols] = gate
        up_v[:, cols] = up
        hid[:, cols] = (gate / (1.0 + jnp.exp(-gate)) * up).astype(jnp.bfloat16)

    tiles(hidden, hidden_step)
    loads[2].wait()

    for i in range(halves):
        def down_step(cols, size, i=i):
            at = pl.ds(pl.multiple_of(cols.start + i * width, size), size)
            part = dot(hid[...], wd[:, at])
            osend[i, :, :, cols] = part.reshape(n, tok, size).astype(jnp.bfloat16)

        tiles(width, down_step)

    for k, (de, dh) in enumerate(everyone):
        pe, ph = wrap(e, de, n), wrap(h, dh, halves)
        c = remote(osend.at[ph, pe], xrecv.at[h, e], out_ss.at[k], out_rs.at[h, e], pe, ph)
        c.start()
        sends.append(c)
    xrecv[h, e] = osend[h, e]

    probs = probs_ref[...]
    shares = probs / jnp.sum(probs, axis=1, keepdims=True)
    ids = ids_ref[...]
    for de, dh in everyone:
        pe, ph = wrap(e, n - de, n), wrap(h, halves - dh, halves)
        slot = xrecv.at[ph, pe]
        remote(slot, slot, out_ss.at[0], out_rs.at[ph, pe], sibling, h).wait_recv()

    layer = jnp.zeros((tok, width), jnp.float32)
    share_rows = []
    for i in range(n):
        total = xrecv[0, i].astype(jnp.float32)
        for j in range(1, halves):
            total = total + xrecv[j, i].astype(jnp.float32)
        named = jnp.sum((ids == i).astype(jnp.float32), axis=1, keepdims=True)
        share = jnp.sum(jnp.where(ids == i, shares, 0.0), axis=1, keepdims=True)
        value = jnp.where(named > 0.0, total, 0.0).astype(jnp.bfloat16)
        xs[i] = value
        layer = layer + share * value.astype(jnp.float32)
        share_rows.append(share)
    layer_ref[...] = layer.astype(jnp.bfloat16)

    x_all = xs[...].reshape(rows, width)
    same = (
        lax.rem(lax.broadcasted_iota(jnp.int32, (tok, rows), 1), tok)
        == lax.broadcasted_iota(jnp.int32, (tok, rows), 0)
    ).astype(jnp.float32)
    gram = dot_t(x_all, x_all).reshape(n, tok, rows) * same[None]
    gram_s[h] = jnp.sum(gram, axis=1)
    for dh in range(1, halves):
        c = remote(
            gram_s.at[h], gram_s.at[h], gram_ss.at[dh], gram_rs.at[h], e, wrap(h, dh, halves)
        )
        c.start()
        sends.append(c)
    for dh in range(1, halves):
        ph = wrap(h, halves - dh, halves)
        slot = gram_s.at[ph]
        remote(slot, slot, gram_ss.at[0], gram_rs.at[ph], e, ph).wait_recv()
    whole = gram_s[0]
    for i in range(1, halves):
        whole = whole + gram_s[i]
    apart = (
        lax.div(lax.broadcasted_iota(jnp.int32, (n, rows), 1), tok)
        != lax.broadcasted_iota(jnp.int32, (n, rows), 0)
    ).astype(jnp.float32)
    whole = whole * (apart * (orth_weight / math.sqrt(full)))
    coeffs = (whole[:, None, :] * same[None]).reshape(rows, rows)
    high = coeffs.astype(jnp.bfloat16)
    low = (coeffs - high.astype(jnp.float32)).astype(jnp.bfloat16)
    pad = pad_ref[...].astype(jnp.float32)

    def grad_step(cols, size):
        x = xs[:, :, cols].reshape(rows, size)
        mixed = (dot(high, x) + dot(low, x)).reshape(n, tok, size)
        upstream = up_ref[:, cols].astype(jnp.float32)
        for i in range(n):
            gsend[i, :, cols] = (pad * (share_rows[i] * upstream + mixed[i])).astype(jnp.bfloat16)

    tiles(width, grad_step)

    for k, (de, dh) in enumerate(everyone):
        pe, ph = wrap(e, de, n), wrap(h, dh, halves)
        c = remote(gsend.at[pe], grows.at[h, e], grad_ss.at[k], grad_rs.at[h, e], pe, ph)
        c.start()
        sends.append(c)
    grows[h, e] = gsend[e]
    for de, dh in everyone:
        pe, ph = wrap(e, n - de, n), wrap(h, halves - dh, halves)
        slot = grows.at[ph, pe]
        remote(slot, slot, grad_ss.at[0], grad_rs.at[ph, pe], sibling, h).wait_recv()

    def act_step(cols, size):
        act = jnp.zeros((rows, size), jnp.float32)
        for i in range(halves):
            g = grows[i].reshape(rows, width)
            act = act + dot_t(g, wd[cols, i * width:(i + 1) * width])
        gate = gate_v[:, cols]
        sigma = 1.0 / (1.0 + jnp.exp(-gate))
        gg[:, cols] = (
            act * up_v[:, cols] * sigma * (1.0 + gate * (1.0 - sigma))
        ).astype(jnp.bfloat16)
        gu[:, cols] = (act * gate * sigma).astype(jnp.bfloat16)

    tiles(hidden, act_step)

    for i in range(halves):
        def back_step(cols, size, i=i):
            at = pl.ds(pl.multiple_of(cols.start + i * width, size), size)
            part = dot_t(gg[...], wg[at, :]) + dot_t(gu[...], wu[at, :])
            part = part.astype(jnp.bfloat16).reshape(chips, 2, tok, size)
            for q in range(2):
                psend[q, i, :, :, cols] = part[:, q]

        tiles(width, back_step)

    c = remote(psend.at[1 - parity], prec, pair_ss, pair_rs, sibling, h)
    c.start()
    sends.append(c)
    c.wait_recv()
    for i in range(halves):
        for m in range(chips):
            rsend[i, m] = (
                psend[parity, i, m].astype(jnp.float32) + prec[i, m].astype(jnp.float32)
            ).astype(jnp.bfloat16)
    for k, (dm, dh) in enumerate(far):
        pm, ph = wrap(chip, dm, chips), wrap(h, dh, halves)
        c = remote(
            rsend.at[ph, pm], fin.at[h, chip], fin_ss.at[k], fin_rs.at[h, chip],
            2 * pm + parity, ph,
        )
        c.start()
        sends.append(c)
    fin[h, chip] = rsend[h, chip]
    for dm, dh in far:
        pm, ph = wrap(chip, chips - dm, chips), wrap(h, halves - dh, halves)
        slot = fin.at[ph, pm]
        remote(slot, slot, fin_ss.at[0], fin_rs.at[ph, pm], sibling, h).wait_recv()
    total = jnp.zeros((tok, width), jnp.float32)
    for i in range(halves):
        for m in range(chips):
            total = total + fin[i, m].astype(jnp.float32)
    gtok_ref[...] = total.astype(jnp.bfloat16)
    for c in sends:
        c.wait_send()


def fused(tokens, upstream, expert_ids, gate_probs, pad_mask, gate_weight, up_weight, down_weight):
    n, halves = lax.axis_size("expert"), lax.axis_size("half")
    tok, width = tokens.shape
    hidden = gate_weight.shape[2]
    rows, full, chips = n * tok, halves * width, n // 2
    low, wide = jnp.bfloat16, jnp.float32
    vmem, dma = pltpu.VMEM, pltpu.SemaphoreType.DMA
    local = pl.BlockSpec(memory_space=pltpu.VMEM)
    remain = pl.BlockSpec(memory_space=pl.ANY)
    return pl.pallas_call(
        functools.partial(fused_kernel, n, halves),
        out_shape=[jax.ShapeDtypeStruct((tok, width), low)] * 2,
        in_specs=[local] * 5 + [remain] * 3,
        out_specs=[local] * 2,
        scratch_shapes=[
            vmem((halves, n, tok, width), low),
            vmem((full, hidden), low),
            vmem((full, hidden), low),
            vmem((hidden, full), low),
            vmem((rows, hidden), wide),
            vmem((rows, hidden), wide),
            vmem((rows, hidden), low),
            vmem((rows, hidden), low),
            vmem((rows, hidden), low),
            vmem((halves, n, tok, width), low),
            vmem((halves, n, tok, width), low),
            vmem((n, tok, width), low),
            vmem((halves, n, rows), wide),
            vmem((n, tok, width), low),
            vmem((halves, n, tok, width), low),
            vmem((2, halves, chips, tok, width), low),
            vmem((halves, chips, tok, width), low),
            vmem((halves, chips, tok, width), low),
            vmem((halves, chips, tok, width), low),
            dma((3,)),
            dma((halves * n,)),
            dma((halves, n)),
            dma((halves * n,)),
            dma((halves, n)),
            dma((halves,)),
            dma((halves,)),
            dma((halves * n,)),
            dma((halves, n)),
            dma,
            dma,
            dma((halves * chips,)),
            dma((halves, chips)),
        ],
        compiler_params=pltpu.CompilerParams(
            collective_id=0, has_side_effects=True, vmem_limit_bytes=56 * 1024 * 1024
        ),
        name="experts",
    )(
        tokens, upstream, expert_ids, gate_probs, pad_mask.reshape(tok, 1),
        gate_weight, up_weight, down_weight,
    )


def shards(tokens, upstream, expert_ids, gate_probs, pad_mask, gate_weight, up_weight, down_weight):
    tok_count, top_count = expert_ids.shape
    experts = lax.axis_size("expert")
    capacity = min(tok_count, 2 * tok_count * top_count // experts)
    if capacity == tok_count and experts % 2 == 0:
        return fused(
            tokens, upstream, expert_ids, gate_probs, pad_mask, gate_weight, up_weight, down_weight
        )
    slots_total = experts * capacity
    full_width = tokens.shape[1] * lax.axis_size("half")
    slot_dest = assign_slots(expert_ids, experts, capacity)
    place_items = placement_matrix(slot_dest, slots_total)
    place_tokens = jnp.sum(place_items.reshape(slots_total, tok_count, top_count), axis=2)
    weight_gate = gate_weight[0]
    weight_up = up_weight[0]
    weight_down = down_weight[0]
    rows_in = to_experts(place_tokens, tokens)
    gate_val = jnp.dot(rows_in, weight_gate, preferred_element_type=jnp.float32)
    up_val = jnp.dot(rows_in, weight_up, preferred_element_type=jnp.float32)
    hidden_act = (jax.nn.silu(gate_val) * up_val).astype(jnp.bfloat16)
    partial_value = jnp.dot(hidden_act, weight_down, preferred_element_type=jnp.float32)
    out_home = to_homes(partial_value)
    outputs = jnp.take(out_home, slot_dest, axis=0).reshape(tok_count, top_count, -1)
    out_float = outputs.astype(jnp.float32)
    shares = gate_probs / jnp.sum(gate_probs, axis=1, keepdims=True)
    layer_out = jnp.sum(shares[:, :, None] * out_float, axis=1).astype(jnp.bfloat16)
    gram_part = jnp.einsum("tjd,tkd->tjk", out_float, out_float) / math.sqrt(full_width)
    gram = lax.psum(gram_part, "half")
    off_diag = 1.0 - jnp.eye(top_count, dtype=jnp.float32)
    coeffs = orth_weight * gram * off_diag
    grad_out = pad_mask.astype(jnp.float32)[:, None, None] * (
        shares[:, :, None] * upstream.astype(jnp.float32)[:, None, :]
        + jnp.einsum("tjk,tkd->tjd", coeffs, out_float)
    )
    grad_items = grad_out.astype(jnp.bfloat16).reshape(tok_count * top_count, -1)
    grad_rows = to_experts(place_items, grad_items)
    grad_act = jnp.einsum("rd,hd->rh", grad_rows, weight_down, preferred_element_type=jnp.float32)
    sigma = jax.nn.sigmoid(gate_val)
    grad_gate = (grad_act * up_val * sigma * (1.0 + gate_val * (1.0 - sigma))).astype(jnp.bfloat16)
    grad_up = (grad_act * gate_val * sigma).astype(jnp.bfloat16)
    grad_partial = jnp.einsum(
        "rh,dh->rd", grad_gate, weight_gate, preferred_element_type=jnp.float32
    )
    grad_partial = grad_partial + jnp.einsum(
        "rh,dh->rd", grad_up, weight_up, preferred_element_type=jnp.float32
    )
    grad_home = to_homes(grad_partial)
    grad_pairs = jnp.take(grad_home, slot_dest, axis=0).reshape(tok_count, top_count, -1)
    grad_tokens = jnp.sum(grad_pairs.astype(jnp.float32), axis=1).astype(jnp.bfloat16)
    return (layer_out, grad_tokens)


def solution(mesh):
    in_specs = (
        P("expert", "half"),
        P("expert", "half"),
        P("expert", None),
        P("expert", None),
        P("expert"),
        P("expert", None, "half"),
        P("expert", None, "half"),
        P("expert", "half", None),
    )
    out_specs = (P("expert", "half"), P("expert", "half"))
    return jax.shard_map(shards, mesh=mesh, in_specs=in_specs, out_specs=out_specs, check_vma=False)
```

```python
import functools
import math

import jax
import jax.numpy as jnp
from jax import lax
from jax.experimental import pallas as pl
from jax.experimental.pallas import tpu as pltpu
from jax.sharding import PartitionSpec as P

orth_weight = 0.25


def assign_slots(expert_ids, experts, capacity):
    tok_count, top_count = expert_ids.shape
    flat_ids = expert_ids.reshape(tok_count * top_count)
    onehot = (flat_ids[:, None] == jnp.arange(experts, dtype=jnp.int32)[None, :]).astype(jnp.int32)
    before = jnp.cumsum(onehot, axis=0) - onehot
    slot_index = jnp.sum(before * onehot, axis=1)
    return flat_ids * capacity + slot_index


def placement_matrix(slot_dest, slots_total):
    row_index = jnp.arange(slots_total, dtype=jnp.int32)
    return (row_index[:, None] == slot_dest[None, :]).astype(jnp.bfloat16)


def to_experts(place, items):
    whole = lax.all_gather(items, "half", axis=1, tiled=True)
    buckets = jnp.dot(place, whole, preferred_element_type=jnp.float32).astype(jnp.bfloat16)
    return lax.all_to_all(buckets, "expert", split_axis=0, concat_axis=0, tiled=True)


def to_homes(partial_value):
    summed = lax.psum_scatter(
        partial_value.astype(jnp.bfloat16), "half", scatter_dimension=1, tiled=True
    )
    return lax.all_to_all(summed, "expert", split_axis=0, concat_axis=0, tiled=True)


def block_of(width):
    return next((b for b in (256, 128) if width % b == 0), width)


def tiles(width, body):
    size = block_of(width)

    def step(j, carry):
        body(pl.ds(pl.multiple_of(j * size, size), size), size)
        return carry

    lax.fori_loop(0, width // size, step, 0)


def dot(a, b):
    return jnp.dot(a, b, preferred_element_type=jnp.float32)


def dot_t(a, b):
    return lax.dot_general(a, b, (((1,), (1,)), ((), ())), preferred_element_type=jnp.float32)


def copy_kernel(a_ref, b_ref, a_out, b_out):
    a_out[...] = a_ref[...]
    b_out[...] = b_ref[...]


def fused_kernel(
    n, halves,
    tok_hbm, up_hbm, ids_hbm, probs_hbm, pad_hbm, wg_hbm, wu_hbm, wd_hbm,
    layer_ref, gtok_ref,
    up_ref, ids_ref, probs_ref, pad_ref,
    tok_buf, wg, wu, wd, gate_v, up_v, hid, gg, gu,
    osend, orecv, ored, xrecv, xs, gram_s, gsend, grows, psend, prec, fsend, frecv, rsend, fin,
    w_sem, tok_ss, tok_rs, part_ss, part_rs, out_ss, out_rs, gram_ss, gram_rs,
    grad_ss, grad_rs, relay_ss, pair_ss, pair_rs, fpart_ss, fpart_rs, fin_ss, fin_rs,
):
    e = lax.axis_index("expert")
    h = lax.axis_index("half")
    tok, width = up_ref.shape
    hidden = wg.shape[1]
    rows = n * tok
    chips = n // 2
    parity = lax.rem(e, 2)
    chip = lax.div(e, 2)
    sibling = e + 1 - 2 * parity
    full = halves * width

    def remote(src, dst, ssem, rsem, pe, ph):
        return pltpu.make_async_remote_copy(
            src_ref=src, dst_ref=dst, send_sem=ssem, recv_sem=rsem,
            device_id=(pe, ph), device_id_type=pl.DeviceIdType.MESH,
        )

    def wrap(a, d, size):
        return lax.rem(a + d, size)

    def arrived(slot, rsem):
        remote(slot, slot, pair_ss.at[0], rsem, sibling, h).wait_recv()

    sends = []

    def send(*args):
        c = remote(*args)
        c.start()
        sends.append(c)

    moves = (
        (tok_hbm, tok_buf.at[h, e]), (ids_hbm, ids_ref), (probs_hbm, probs_ref),
        (pad_hbm, pad_ref), (up_hbm, up_ref),
        (wg_hbm.at[0], wg), (wu_hbm.at[0], wu), (wd_hbm.at[0], wd),
    )
    loads = [pltpu.make_async_copy(src, dst, w_sem.at[i]) for i, (src, dst) in enumerate(moves)]
    for c in loads:
        c.start()

    others = list(range(1, halves))
    near = sorted(range(1, n), key=lambda d: (min(d, n - d), d))
    outer = near[::-1]
    chips_near = sorted(range(1, chips), key=lambda d: (min(d, chips - d), d))
    chips_far = chips_near[::-1]

    barrier = pltpu.get_barrier_semaphore()
    for d in outer:
        pl.semaphore_signal(
            barrier, inc=1, device_id=(wrap(e, d, n), h), device_id_type=pl.DeviceIdType.MESH
        )
    for d in others:
        pl.semaphore_signal(
            barrier, inc=1, device_id=(e, wrap(h, d, halves)), device_id_type=pl.DeviceIdType.MESH
        )
    pl.semaphore_wait(barrier, len(outer) + len(others))

    loads[0].wait()
    k = 0
    mine = tok_buf.at[h, e]
    for d in chips_far:
        send(mine, mine, tok_ss.at[k], tok_rs.at[h, e], 2 * wrap(chip, d, chips) + parity, h)
        k += 1
    for d in others:
        send(mine, mine, tok_ss.at[k], tok_rs.at[h, e], e, wrap(h, d, halves))
        k += 1
    send(mine, mine, tok_ss.at[k], tok_rs.at[h, e], sibling, h)
    k += 1
    for d in chips_near:
        pe = 2 * wrap(chip, chips - d, chips) + parity
        slot = tok_buf.at[h, pe]
        arrived(slot, tok_rs.at[h, pe])
        for dh in others:
            send(slot, slot, tok_ss.at[k], tok_rs.at[h, pe], e, wrap(h, dh, halves))
            k += 1
        send(slot, slot, tok_ss.at[k], tok_rs.at[h, pe], sibling, h)
        k += 1
    for d in [0] + chips_near:
        pe = 2 * wrap(chip, chips - d, chips) + parity
        for dh in others:
            ph = wrap(h, halves - dh, halves)
            slot = tok_buf.at[ph, pe]
            arrived(slot, tok_rs.at[ph, pe])
            send(slot, slot, tok_ss.at[k], tok_rs.at[ph, pe], sibling, h)
            k += 1
    for c in loads[1:7]:
        c.wait()
    for d in [0] + chips_near:
        pe = 2 * wrap(chip, chips - d, chips) + 1 - parity
        for ph in range(halves):
            arrived(tok_buf.at[ph, pe], tok_rs.at[ph, pe])

    def hidden_step(cols, size):
        gate = jnp.zeros((rows, size), jnp.float32)
        up = jnp.zeros((rows, size), jnp.float32)
        for i in range(halves):
            x = tok_buf[i].reshape(rows, width)
            gate = gate + dot(x, wg[i * width:(i + 1) * width, cols])
            up = up + dot(x, wu[i * width:(i + 1) * width, cols])
        gate_v[:, cols] = gate
        up_v[:, cols] = up
        hid[:, cols] = (gate / (1.0 + jnp.exp(-gate)) * up).astype(jnp.bfloat16)

    tiles(hidden, hidden_step)
    loads[7].wait()

    for dh in others + [0]:
        ph = wrap(h, dh, halves)

        def down_step(cols, size, ph=ph, dh=dh):
            at = pl.ds(pl.multiple_of(cols.start + ph * width, size), size)
            part = dot(hid[...], wd[:, at])
            osend[dh, :, :, cols] = part.reshape(n, tok, size).astype(jnp.bfloat16)

        tiles(width, down_step)
        if dh:
            for j, d in enumerate(outer + [0]):
                pe = wrap(e, d, n)
                send(
                    osend.at[dh, pe], orecv.at[halves - dh, pe],
                    part_ss.at[dh, j], part_rs.at[halves - dh, j], e, ph,
                )

    eye = (
        lax.broadcasted_iota(jnp.int32, (tok, tok), 0)
        == lax.broadcasted_iota(jnp.int32, (tok, tok), 1)
    )
    top = ids_ref.shape[0]
    lane = lax.broadcasted_iota(jnp.int32, (tok, top), 1)

    def column(row):
        return jnp.sum(jnp.where(eye, jnp.broadcast_to(row, (tok, tok)), 0.0), axis=1, keepdims=True)

    ids = jnp.zeros((tok, top), jnp.float32)
    probs = jnp.zeros((tok, top), jnp.float32)
    for j in range(top):
        ids = jnp.where(lane == j, column(ids_ref[j:j + 1, :].astype(jnp.float32)), ids)
        probs = jnp.where(lane == j, column(probs_ref[j:j + 1, :]), probs)
    pad = column(pad_ref[...].astype(jnp.float32))
    shares = probs / jnp.sum(probs, axis=1, keepdims=True)
    named_rows, share_rows = [], []
    for i in range(n):
        named_rows.append(jnp.sum((ids == float(i)).astype(jnp.float32), axis=1, keepdims=True))
        share_rows.append(jnp.sum(jnp.where(ids == float(i), shares, 0.0), axis=1, keepdims=True))

    for j, d in enumerate(outer + [0]):
        pe = wrap(e, d, n)
        total = osend[0, pe].astype(jnp.float32)
        for dh in others:
            arrived(orecv.at[dh, pe], part_rs.at[dh, j])
            total = total + orecv[dh, pe].astype(jnp.float32)
        if d:
            ored[pe] = total.astype(jnp.bfloat16)
            send(ored.at[pe], xrecv.at[e], out_ss.at[j], out_rs.at[e], pe, h)
        else:
            xrecv[e] = total.astype(jnp.bfloat16)
    for d in near:
        pe = wrap(e, n - d, n)
        arrived(xrecv.at[pe], out_rs.at[pe])

    layer = jnp.zeros((tok, width), jnp.float32)
    for i in range(n):
        value = xrecv[i]
        value = jnp.where(named_rows[i] > 0.0, value.astype(jnp.float32), 0.0)
        xs[i] = value.astype(jnp.bfloat16)
        layer = layer + share_rows[i] * value
    layer_ref[...] = layer.astype(jnp.bfloat16)

    x_all = xs[...].reshape(rows, width)
    same = (
        lax.rem(lax.broadcasted_iota(jnp.int32, (tok, rows), 1), tok)
        == lax.broadcasted_iota(jnp.int32, (tok, rows), 0)
    ).astype(jnp.float32)
    gram = dot_t(x_all, x_all).reshape(n, tok, rows) * same[None]
    gram_s[h] = jnp.sum(gram, axis=1)
    for dh in range(1, halves):
        send(gram_s.at[h], gram_s.at[h], gram_ss.at[dh], gram_rs.at[h], e, wrap(h, dh, halves))
    for dh in range(1, halves):
        ph = wrap(h, halves - dh, halves)
        arrived(gram_s.at[ph], gram_rs.at[ph])
    whole = gram_s[0]
    for i in range(1, halves):
        whole = whole + gram_s[i]
    apart = (
        lax.div(lax.broadcasted_iota(jnp.int32, (n, rows), 1), tok)
        != lax.broadcasted_iota(jnp.int32, (n, rows), 0)
    ).astype(jnp.float32)
    whole = whole * (apart * (orth_weight / math.sqrt(full)))
    coeffs = (whole[:, None, :] * same[None]).reshape(rows, rows)
    high = coeffs.astype(jnp.bfloat16)
    low = (coeffs - high.astype(jnp.float32)).astype(jnp.bfloat16)

    def grad_step(cols, size):
        x = xs[:, :, cols].reshape(rows, size)
        mixed = (dot(high, x) + dot(low, x)).reshape(n, tok, size)
        upstream = up_ref[:, cols].astype(jnp.float32)
        for i in range(n):
            gsend[i, :, cols] = (pad * (share_rows[i] * upstream + mixed[i])).astype(jnp.bfloat16)

    tiles(width, grad_step)

    for j, d in enumerate(outer):
        pe = wrap(e, d, n)
        send(gsend.at[pe], grows.at[h, e], grad_ss.at[j], grad_rs.at[h, e], pe, h)
    k = 0
    for dh in others:
        send(gsend.at[e], grows.at[h, e], relay_ss.at[k], grad_rs.at[h, e], e, wrap(h, dh, halves))
        k += 1
    grows[h, e] = gsend[e]
    for d in near:
        pe = wrap(e, n - d, n)
        slot = grows.at[h, pe]
        arrived(slot, grad_rs.at[h, pe])
        for dh in others:
            send(slot, slot, relay_ss.at[k], grad_rs.at[h, pe], e, wrap(h, dh, halves))
            k += 1
    for d in [0] + near:
        pe = wrap(e, n - d, n)
        for dh in others:
            ph = wrap(h, halves - dh, halves)
            arrived(grows.at[ph, pe], grad_rs.at[ph, pe])

    def act_step(cols, size):
        act = jnp.zeros((rows, size), jnp.float32)
        for i in range(halves):
            g = grows[i].reshape(rows, width)
            act = act + dot_t(g, wd[cols, i * width:(i + 1) * width])
        gate = gate_v[:, cols]
        sigma = 1.0 / (1.0 + jnp.exp(-gate))
        gg[:, cols] = (
            act * up_v[:, cols] * sigma * (1.0 + gate * (1.0 - sigma))
        ).astype(jnp.bfloat16)
        gu[:, cols] = (act * gate * sigma).astype(jnp.bfloat16)

    tiles(hidden, act_step)

    for dh in others + [0]:
        ph = wrap(h, dh, halves)

        def back_step(cols, size, ph=ph, dh=dh):
            at = pl.ds(pl.multiple_of(cols.start + ph * width, size), size)
            part = dot_t(gg[...], wg[at, :]) + dot_t(gu[...], wu[at, :])
            part = part.astype(jnp.bfloat16).reshape(chips, 2, tok, size)
            for q in range(2):
                psend[dh, q, :, :, cols] = part[:, q]

        tiles(width, back_step)
        send(psend.at[dh, 1 - parity], prec.at[dh], pair_ss.at[dh], pair_rs.at[dh], sibling, h)
    order = chips_far + [0]
    for dh in others:
        arrived(prec.at[dh], pair_rs.at[dh])
        for j, d in enumerate(order):
            pm = wrap(chip, d, chips)
            fsend[dh, pm] = (
                psend[dh, parity, pm].astype(jnp.float32) + prec[dh, pm].astype(jnp.float32)
            ).astype(jnp.bfloat16)
            send(
                fsend.at[dh, pm], frecv.at[halves - dh, pm],
                fpart_ss.at[dh, j], fpart_rs.at[halves - dh, j], e, wrap(h, dh, halves),
            )
    arrived(prec.at[0], pair_rs.at[0])
    for j, d in enumerate(order):
        pm = wrap(chip, d, chips)
        total = psend[0, parity, pm].astype(jnp.float32) + prec[0, pm].astype(jnp.float32)
        for dh in others:
            arrived(frecv.at[dh, pm], fpart_rs.at[dh, j])
            total = total + frecv[dh, pm].astype(jnp.float32)
        if d:
            rsend[pm] = total.astype(jnp.bfloat16)
            send(rsend.at[pm], fin.at[chip], fin_ss.at[j], fin_rs.at[chip], 2 * pm + parity, h)
    for d in chips_near:
        pm = wrap(chip, chips - d, chips)
        arrived(fin.at[pm], fin_rs.at[pm])
        total = total + fin[pm].astype(jnp.float32)
    gtok_ref[...] = total.astype(jnp.bfloat16)
    for c in sends:
        c.wait_send()


def fused(tokens, upstream, expert_ids, gate_probs, pad_mask, gate_weight, up_weight, down_weight):
    n, halves = lax.axis_size("expert"), lax.axis_size("half")
    tok, width = tokens.shape
    hidden = gate_weight.shape[2]
    rows, full, chips = n * tok, halves * width, n // 2
    top = expert_ids.shape[1]
    low, wide = jnp.bfloat16, jnp.float32
    vmem, dma = pltpu.VMEM, pltpu.SemaphoreType.DMA
    local = pl.BlockSpec(memory_space=pltpu.VMEM)
    remain = pl.BlockSpec(memory_space=pl.ANY)
    result = [jax.ShapeDtypeStruct((tok, width), low)] * 2
    outs = pl.pallas_call(
        functools.partial(fused_kernel, n, halves),
        out_shape=result,
        in_specs=[remain] * 8,
        out_specs=[local] * 2,
        scratch_shapes=[
            vmem((tok, width), low),
            vmem((top, tok), jnp.int32),
            vmem((top, tok), wide),
            vmem((1, tok), jnp.int32),
            vmem((halves, n, tok, width), low),
            vmem((full, hidden), low),
            vmem((full, hidden), low),
            vmem((hidden, full), low),
            vmem((rows, hidden), wide),
            vmem((rows, hidden), wide),
            vmem((rows, hidden), low),
            vmem((rows, hidden), low),
            vmem((rows, hidden), low),
            vmem((halves, n, tok, width), low),
            vmem((halves, n, tok, width), low),
            vmem((n, tok, width), low),
            vmem((n, tok, width), low),
            vmem((n, tok, width), low),
            vmem((halves, n, rows), wide),
            vmem((n, tok, width), low),
            vmem((halves, n, tok, width), low),
            vmem((halves, 2, chips, tok, width), low),
            vmem((halves, chips, tok, width), low),
            vmem((halves, chips, tok, width), low),
            vmem((halves, chips, tok, width), low),
            vmem((chips, tok, width), low),
            vmem((chips, tok, width), low),
            dma((8,)),
            dma((2 * halves * n,)),
            dma((halves, n)),
            dma((halves, n)),
            dma((halves, n)),
            dma((n,)),
            dma((n,)),
            dma((halves,)),
            dma((halves,)),
            dma((n,)),
            dma((halves, n)),
            dma((halves * n,)),
            dma((halves,)),
            dma((halves,)),
            dma((halves, chips)),
            dma((halves, chips)),
            dma((chips,)),
            dma((chips,)),
        ],
        compiler_params=pltpu.CompilerParams(
            collective_id=0, has_side_effects=True, vmem_limit_bytes=56 * 1024 * 1024
        ),
        name="experts",
    )(
        tokens, upstream, expert_ids.T, gate_probs.T, pad_mask.reshape(1, tok),
        gate_weight, up_weight, down_weight,
    )
    return pl.pallas_call(
        copy_kernel, out_shape=result, in_specs=[local] * 2, out_specs=[local] * 2, name="results"
    )(*outs)


def shards(tokens, upstream, expert_ids, gate_probs, pad_mask, gate_weight, up_weight, down_weight):
    tok_count, top_count = expert_ids.shape
    experts = lax.axis_size("expert")
    capacity = min(tok_count, 2 * tok_count * top_count // experts)
    if capacity == tok_count and experts % 2 == 0:
        return fused(
            tokens, upstream, expert_ids, gate_probs, pad_mask, gate_weight, up_weight, down_weight
        )
    slots_total = experts * capacity
    full_width = tokens.shape[1] * lax.axis_size("half")
    slot_dest = assign_slots(expert_ids, experts, capacity)
    place_items = placement_matrix(slot_dest, slots_total)
    place_tokens = jnp.sum(place_items.reshape(slots_total, tok_count, top_count), axis=2)
    weight_gate = gate_weight[0]
    weight_up = up_weight[0]
    weight_down = down_weight[0]
    rows_in = to_experts(place_tokens, tokens)
    gate_val = jnp.dot(rows_in, weight_gate, preferred_element_type=jnp.float32)
    up_val = jnp.dot(rows_in, weight_up, preferred_element_type=jnp.float32)
    hidden_act = (jax.nn.silu(gate_val) * up_val).astype(jnp.bfloat16)
    partial_value = jnp.dot(hidden_act, weight_down, preferred_element_type=jnp.float32)
    out_home = to_homes(partial_value)
    outputs = jnp.take(out_home, slot_dest, axis=0).reshape(tok_count, top_count, -1)
    out_float = outputs.astype(jnp.float32)
    shares = gate_probs / jnp.sum(gate_probs, axis=1, keepdims=True)
    layer_out = jnp.sum(shares[:, :, None] * out_float, axis=1).astype(jnp.bfloat16)
    gram_part = jnp.einsum("tjd,tkd->tjk", out_float, out_float) / math.sqrt(full_width)
    gram = lax.psum(gram_part, "half")
    off_diag = 1.0 - jnp.eye(top_count, dtype=jnp.float32)
    coeffs = orth_weight * gram * off_diag
    grad_out = pad_mask.astype(jnp.float32)[:, None, None] * (
        shares[:, :, None] * upstream.astype(jnp.float32)[:, None, :]
        + jnp.einsum("tjk,tkd->tjd", coeffs, out_float)
    )
    grad_items = grad_out.astype(jnp.bfloat16).reshape(tok_count * top_count, -1)
    grad_rows = to_experts(place_items, grad_items)
    grad_act = jnp.einsum("rd,hd->rh", grad_rows, weight_down, preferred_element_type=jnp.float32)
    sigma = jax.nn.sigmoid(gate_val)
    grad_gate = (grad_act * up_val * sigma * (1.0 + gate_val * (1.0 - sigma))).astype(jnp.bfloat16)
    grad_up = (grad_act * gate_val * sigma).astype(jnp.bfloat16)
    grad_partial = jnp.einsum(
        "rh,dh->rd", grad_gate, weight_gate, preferred_element_type=jnp.float32
    )
    grad_partial = grad_partial + jnp.einsum(
        "rh,dh->rd", grad_up, weight_up, preferred_element_type=jnp.float32
    )
    grad_home = to_homes(grad_partial)
    grad_pairs = jnp.take(grad_home, slot_dest, axis=0).reshape(tok_count, top_count, -1)
    grad_tokens = jnp.sum(grad_pairs.astype(jnp.float32), axis=1).astype(jnp.bfloat16)
    return (layer_out, grad_tokens)


def solution(mesh):
    in_specs = (
        P("expert", "half"),
        P("expert", "half"),
        P("expert", None),
        P("expert", None),
        P("expert"),
        P("expert", None, "half"),
        P("expert", None, "half"),
        P("expert", "half", None),
    )
    out_specs = (P("expert", "half"), P("expert", "half"))
    return jax.shard_map(shards, mesh=mesh, in_specs=in_specs, out_specs=out_specs, check_vma=False)
```

```python
import functools
import math

import jax
import jax.numpy as jnp
from jax import lax
from jax.experimental import pallas as pl
from jax.experimental.pallas import tpu as pltpu
from jax.sharding import PartitionSpec as P

orth_weight = 0.25


def assign_slots(expert_ids, experts, capacity):
    tok_count, top_count = expert_ids.shape
    flat_ids = expert_ids.reshape(tok_count * top_count)
    onehot = (flat_ids[:, None] == jnp.arange(experts, dtype=jnp.int32)[None, :]).astype(jnp.int32)
    before = jnp.cumsum(onehot, axis=0) - onehot
    slot_index = jnp.sum(before * onehot, axis=1)
    return flat_ids * capacity + slot_index


def placement_matrix(slot_dest, slots_total):
    row_index = jnp.arange(slots_total, dtype=jnp.int32)
    return (row_index[:, None] == slot_dest[None, :]).astype(jnp.bfloat16)


def to_experts(place, items):
    whole = lax.all_gather(items, "half", axis=1, tiled=True)
    buckets = jnp.dot(place, whole, preferred_element_type=jnp.float32).astype(jnp.bfloat16)
    return lax.all_to_all(buckets, "expert", split_axis=0, concat_axis=0, tiled=True)


def to_homes(partial_value):
    summed = lax.psum_scatter(
        partial_value.astype(jnp.bfloat16), "half", scatter_dimension=1, tiled=True
    )
    return lax.all_to_all(summed, "expert", split_axis=0, concat_axis=0, tiled=True)


def block_of(width):
    return next((b for b in (256, 128) if width % b == 0), width)


def tiles(width, body):
    size = block_of(width)

    def step(j, carry):
        body(pl.ds(pl.multiple_of(j * size, size), size), size)
        return carry

    lax.fori_loop(0, width // size, step, 0)


def dot(a, b):
    return jnp.dot(a, b, preferred_element_type=jnp.float32)


def dot_t(a, b):
    return lax.dot_general(a, b, (((1,), (1,)), ((), ())), preferred_element_type=jnp.float32)


def copy_kernel(a_ref, b_ref, a_out, b_out):
    a_out[...] = a_ref[...]
    b_out[...] = b_ref[...]


def fused_kernel(
    n, halves,
    tok_hbm, up_hbm, ids_hbm, probs_hbm, pad_hbm, wg_hbm, wu_hbm, wd_hbm,
    layer_ref, gtok_ref,
    up_ref, ids_ref, probs_ref, pad_ref,
    tok_buf, wg, wu, wd, gate_v, up_v, hid, gg, gu,
    osend, orecv, ored, xrecv, xs, gram_s, whole_s, gsend, grows, psend, prec, fsend, frecv, rsend, fin,
    w_sem, tok_ss, tok_rs, part_ss, part_rs, out_ss, out_rs, gram_ss, gram_rs,
    grad_ss, grad_rs, relay_ss, pair_ss, pair_rs, fpart_ss, fpart_rs, fin_ss, fin_rs,
):
    e = lax.axis_index("expert")
    h = lax.axis_index("half")
    tok, width = up_ref.shape
    hidden = wg.shape[1]
    rows = n * tok
    chips = n // 2
    group = min(n, 8)
    parity = lax.rem(e, 2)
    chip = lax.div(e, 2)
    sibling = e + 1 - 2 * parity
    full = halves * width

    def remote(src, dst, ssem, rsem, pe, ph):
        return pltpu.make_async_remote_copy(
            src_ref=src, dst_ref=dst, send_sem=ssem, recv_sem=rsem,
            device_id=(pe, ph), device_id_type=pl.DeviceIdType.MESH,
        )

    def wrap(a, d, size):
        return lax.rem(a + d, size)

    def flip(a, d):
        bit = 1
        out = a
        while bit <= d:
            if d & bit:
                out = out + bit * (1 - 2 * lax.rem(lax.div(a, bit), 2))
            bit *= 2
        return out

    def arrived(slot, rsem):
        remote(slot, slot, pair_ss.at[0], rsem, sibling, h).wait_recv()

    sends = []

    def send(*args):
        c = remote(*args)
        c.start()
        sends.append(c)

    moves = (
        (tok_hbm, tok_buf.at[h, e]), (ids_hbm, ids_ref), (probs_hbm, probs_ref),
        (pad_hbm, pad_ref), (up_hbm, up_ref),
        (wg_hbm.at[0], wg), (wu_hbm.at[0], wu), (wd_hbm.at[0], wd),
    )
    loads = [pltpu.make_async_copy(src, dst, w_sem.at[i]) for i, (src, dst) in enumerate(moves)]
    for c in loads:
        c.start()

    others = list(range(1, halves))
    near = list(range(1, n))
    outer = near[::-1]
    chips_near = list(range(1, chips))
    chips_far = chips_near[::-1]

    barrier = pltpu.get_barrier_semaphore()
    for d in outer:
        pl.semaphore_signal(
            barrier, inc=1, device_id=(flip(e, d), h), device_id_type=pl.DeviceIdType.MESH
        )
    for d in others:
        pl.semaphore_signal(
            barrier, inc=1, device_id=(e, wrap(h, d, halves)), device_id_type=pl.DeviceIdType.MESH
        )
    pl.semaphore_wait(barrier, len(outer) + len(others))

    loads[0].wait()
    k = 0
    mine = tok_buf.at[h, e]
    for d in chips_far:
        send(mine, mine, tok_ss.at[k], tok_rs.at[h, e], 2 * flip(chip, d) + parity, h)
        k += 1
    for d in others:
        send(mine, mine, tok_ss.at[k], tok_rs.at[h, e], e, wrap(h, d, halves))
        k += 1
    send(mine, mine, tok_ss.at[k], tok_rs.at[h, e], sibling, h)
    k += 1
    for d in chips_near:
        pe = 2 * flip(chip, d) + parity
        slot = tok_buf.at[h, pe]
        arrived(slot, tok_rs.at[h, pe])
        for dh in others:
            send(slot, slot, tok_ss.at[k], tok_rs.at[h, pe], e, wrap(h, dh, halves))
            k += 1
        send(slot, slot, tok_ss.at[k], tok_rs.at[h, pe], sibling, h)
        k += 1
    for d in [0] + chips_near:
        pe = 2 * flip(chip, d) + parity
        for dh in others:
            ph = wrap(h, halves - dh, halves)
            slot = tok_buf.at[ph, pe]
            arrived(slot, tok_rs.at[ph, pe])
            send(slot, slot, tok_ss.at[k], tok_rs.at[ph, pe], sibling, h)
            k += 1
    for c in loads[1:7]:
        c.wait()
    for d in [0] + chips_near:
        pe = 2 * flip(chip, d) + 1 - parity
        for ph in range(halves):
            arrived(tok_buf.at[ph, pe], tok_rs.at[ph, pe])

    def hidden_step(cols, size):
        gate = jnp.zeros((rows, size), jnp.float32)
        up = jnp.zeros((rows, size), jnp.float32)
        for i in range(halves):
            x = tok_buf[i].reshape(rows, width)
            gate = gate + dot(x, wg[i * width:(i + 1) * width, cols])
            up = up + dot(x, wu[i * width:(i + 1) * width, cols])
        gate_v[:, cols] = gate
        up_v[:, cols] = up
        hid[:, cols] = (gate / (1.0 + jnp.exp(-gate)) * up).astype(jnp.bfloat16)

    tiles(hidden, hidden_step)
    loads[7].wait()

    for dh in others + [0]:
        ph = wrap(h, dh, halves)

        def down_step(cols, size, ph=ph, dh=dh):
            at = pl.ds(pl.multiple_of(cols.start + ph * width, size), size)
            part = dot(hid[...], wd[:, at])
            osend[dh, :, :, cols] = part.reshape(n, tok, size).astype(jnp.bfloat16)

        tiles(width, down_step)
        if dh:
            for j, d in enumerate(outer + [0]):
                pe = flip(e, d)
                send(
                    osend.at[dh, pe], orecv.at[halves - dh, pe],
                    part_ss.at[dh, j], part_rs.at[halves - dh, j], e, ph,
                )

    eye = (
        lax.broadcasted_iota(jnp.int32, (tok, tok), 0)
        == lax.broadcasted_iota(jnp.int32, (tok, tok), 1)
    )
    top = ids_ref.shape[0]
    lane = lax.broadcasted_iota(jnp.int32, (tok, top), 1)

    def column(row):
        return jnp.sum(jnp.where(eye, jnp.broadcast_to(row, (tok, tok)), 0.0), axis=1, keepdims=True)

    ids = jnp.zeros((tok, top), jnp.float32)
    probs = jnp.zeros((tok, top), jnp.float32)
    for j in range(top):
        ids = jnp.where(lane == j, column(ids_ref[j:j + 1, :].astype(jnp.float32)), ids)
        probs = jnp.where(lane == j, column(probs_ref[j:j + 1, :]), probs)
    pad = column(pad_ref[...].astype(jnp.float32))
    shares = probs / jnp.sum(probs, axis=1, keepdims=True)
    for j, d in enumerate(outer + [0]):
        pe = flip(e, d)
        total = osend[0, pe].astype(jnp.float32)
        for dh in others:
            arrived(orecv.at[dh, pe], part_rs.at[dh, j])
            total = total + orecv[dh, pe].astype(jnp.float32)
        if d:
            ored[pe] = total.astype(jnp.bfloat16)
            send(ored.at[pe], xrecv.at[e], out_ss.at[j], out_rs.at[e], pe, h)
        else:
            xrecv[e] = total.astype(jnp.bfloat16)
    def share_of(i):
        listed = (ids == i.astype(jnp.float32)).astype(jnp.float32)
        return jnp.sum(listed * shares, axis=1, keepdims=True), jnp.sum(listed, axis=1, keepdims=True)

    layer = jnp.zeros((tok, width), jnp.float32)
    for d in [0] + near:
        pe = flip(e, d)
        share, listed = share_of(pe)
        if d:
            arrived(xrecv.at[pe], out_rs.at[pe])
        value = jnp.where(listed > 0.0, xrecv[pe].astype(jnp.float32), 0.0)
        xs[pe] = value.astype(jnp.bfloat16)
        layer = layer + share * value

    x_all = xs[...].reshape(rows, width)
    same = (
        lax.rem(lax.broadcasted_iota(jnp.int32, (tok, rows), 1), tok)
        == lax.broadcasted_iota(jnp.int32, (tok, rows), 0)
    ).astype(jnp.float32)
    gram = dot_t(x_all, x_all).reshape(n, tok, rows) * same[None]
    gram_s[h] = jnp.sum(gram, axis=1)
    for dh in range(1, halves):
        send(gram_s.at[h], gram_s.at[h], gram_ss.at[dh], gram_rs.at[h], e, wrap(h, dh, halves))
    for dh in range(1, halves):
        ph = wrap(h, halves - dh, halves)
        arrived(gram_s.at[ph], gram_rs.at[ph])
    whole = gram_s[0]
    for i in range(1, halves):
        whole = whole + gram_s[i]
    apart = (
        lax.div(lax.broadcasted_iota(jnp.int32, (n, rows), 1), tok)
        != lax.broadcasted_iota(jnp.int32, (n, rows), 0)
    ).astype(jnp.float32)
    whole = whole * (apart * (orth_weight / math.sqrt(full)))
    whole_s[...] = whole
    x_all = xs[...].reshape(rows, width)
    upstream = up_ref[...].astype(jnp.float32)
    for g in range(n // group):
        first = pl.multiple_of(flip(lax.div(e, group), g) * group, group)
        coeffs = whole_s[pl.ds(first, group), :][:, None, :] * same[None]
        coeffs = coeffs.reshape(group * tok, rows)
        high = coeffs.astype(jnp.bfloat16)
        low = (coeffs - high.astype(jnp.float32)).astype(jnp.bfloat16)
        mixed = (dot(high, x_all) + dot(low, x_all)).reshape(group, tok, width)
        for i in range(group):
            share, _ = share_of(first + i)
            gsend[first + i] = (pad * (share * upstream + mixed[i])).astype(jnp.bfloat16)
        for d in range(max(1, g * group), (g + 1) * group):
            pe = flip(e, d)
            send(gsend.at[pe], grows.at[h, e], grad_ss.at[d], grad_rs.at[h, e], pe, h)
        if g == 0:
            for dh in others:
                send(
                    gsend.at[e], grows.at[h, e], relay_ss.at[dh - 1], grad_rs.at[h, e],
                    e, wrap(h, dh, halves),
                )
    layer_ref[...] = layer.astype(jnp.bfloat16)
    k = len(others)
    grows[h, e] = gsend[e]
    for d in near:
        pe = flip(e, d)
        slot = grows.at[h, pe]
        arrived(slot, grad_rs.at[h, pe])
        for dh in others:
            send(slot, slot, relay_ss.at[k], grad_rs.at[h, pe], e, wrap(h, dh, halves))
            k += 1
    for d in [0] + near:
        pe = flip(e, d)
        for dh in others:
            ph = wrap(h, halves - dh, halves)
            arrived(grows.at[ph, pe], grad_rs.at[ph, pe])

    def act_step(cols, size):
        act = jnp.zeros((rows, size), jnp.float32)
        for i in range(halves):
            g = grows[i].reshape(rows, width)
            act = act + dot_t(g, wd[cols, i * width:(i + 1) * width])
        gate = gate_v[:, cols]
        sigma = 1.0 / (1.0 + jnp.exp(-gate))
        gg[:, cols] = (
            act * up_v[:, cols] * sigma * (1.0 + gate * (1.0 - sigma))
        ).astype(jnp.bfloat16)
        gu[:, cols] = (act * gate * sigma).astype(jnp.bfloat16)

    tiles(hidden, act_step)

    for dh in others + [0]:
        ph = wrap(h, dh, halves)

        def back_step(cols, size, ph=ph, dh=dh):
            at = pl.ds(pl.multiple_of(cols.start + ph * width, size), size)
            part = dot_t(gg[...], wg[at, :]) + dot_t(gu[...], wu[at, :])
            part = part.astype(jnp.bfloat16).reshape(chips, 2, tok, size)
            for q in range(2):
                psend[dh, q, :, :, cols] = part[:, q]

        tiles(width, back_step)
        send(psend.at[dh, 1 - parity], prec.at[dh], pair_ss.at[dh], pair_rs.at[dh], sibling, h)
    order = chips_far + [0]
    for dh in others:
        arrived(prec.at[dh], pair_rs.at[dh])
        for j, d in enumerate(order):
            pm = flip(chip, d)
            fsend[dh, pm] = (
                psend[dh, parity, pm].astype(jnp.float32) + prec[dh, pm].astype(jnp.float32)
            ).astype(jnp.bfloat16)
            send(
                fsend.at[dh, pm], frecv.at[halves - dh, pm],
                fpart_ss.at[dh, j], fpart_rs.at[halves - dh, j], e, wrap(h, dh, halves),
            )
    arrived(prec.at[0], pair_rs.at[0])
    for j, d in enumerate(order):
        pm = flip(chip, d)
        total = psend[0, parity, pm].astype(jnp.float32) + prec[0, pm].astype(jnp.float32)
        for dh in others:
            arrived(frecv.at[dh, pm], fpart_rs.at[dh, j])
            total = total + frecv[dh, pm].astype(jnp.float32)
        if d:
            rsend[pm] = total.astype(jnp.bfloat16)
            send(rsend.at[pm], fin.at[chip], fin_ss.at[j], fin_rs.at[chip], 2 * pm + parity, h)
    for d in chips_near:
        pm = flip(chip, d)
        arrived(fin.at[pm], fin_rs.at[pm])
        total = total + fin[pm].astype(jnp.float32)
    gtok_ref[...] = total.astype(jnp.bfloat16)
    for c in sends:
        c.wait_send()


def fused(tokens, upstream, expert_ids, gate_probs, pad_mask, gate_weight, up_weight, down_weight):
    n, halves = lax.axis_size("expert"), lax.axis_size("half")
    tok, width = tokens.shape
    hidden = gate_weight.shape[2]
    rows, full, chips = n * tok, halves * width, n // 2
    top = expert_ids.shape[1]
    low, wide = jnp.bfloat16, jnp.float32
    vmem, dma = pltpu.VMEM, pltpu.SemaphoreType.DMA
    local = pl.BlockSpec(memory_space=pltpu.VMEM)
    remain = pl.BlockSpec(memory_space=pl.ANY)
    result = [jax.ShapeDtypeStruct((tok, width), low)] * 2
    outs = pl.pallas_call(
        functools.partial(fused_kernel, n, halves),
        out_shape=result,
        in_specs=[remain] * 8,
        out_specs=[local] * 2,
        scratch_shapes=[
            vmem((tok, width), low),
            vmem((top, tok), jnp.int32),
            vmem((top, tok), wide),
            vmem((1, tok), jnp.int32),
            vmem((halves, n, tok, width), low),
            vmem((full, hidden), low),
            vmem((full, hidden), low),
            vmem((hidden, full), low),
            vmem((rows, hidden), wide),
            vmem((rows, hidden), wide),
            vmem((rows, hidden), low),
            vmem((rows, hidden), low),
            vmem((rows, hidden), low),
            vmem((halves, n, tok, width), low),
            vmem((halves, n, tok, width), low),
            vmem((n, tok, width), low),
            vmem((n, tok, width), low),
            vmem((n, tok, width), low),
            vmem((halves, n, rows), wide),
            vmem((n, rows), wide),
            vmem((n, tok, width), low),
            vmem((halves, n, tok, width), low),
            vmem((halves, 2, chips, tok, width), low),
            vmem((halves, chips, tok, width), low),
            vmem((halves, chips, tok, width), low),
            vmem((halves, chips, tok, width), low),
            vmem((chips, tok, width), low),
            vmem((chips, tok, width), low),
            dma((8,)),
            dma((2 * halves * n,)),
            dma((halves, n)),
            dma((halves, n)),
            dma((halves, n)),
            dma((n,)),
            dma((n,)),
            dma((halves,)),
            dma((halves,)),
            dma((n,)),
            dma((halves, n)),
            dma((halves * n,)),
            dma((halves,)),
            dma((halves,)),
            dma((halves, chips)),
            dma((halves, chips)),
            dma((chips,)),
            dma((chips,)),
        ],
        compiler_params=pltpu.CompilerParams(
            collective_id=0, has_side_effects=True, vmem_limit_bytes=56 * 1024 * 1024
        ),
        name="experts",
    )(
        tokens, upstream, expert_ids.T, gate_probs.T, pad_mask.reshape(1, tok),
        gate_weight, up_weight, down_weight,
    )
    return pl.pallas_call(
        copy_kernel, out_shape=result, in_specs=[local] * 2, out_specs=[local] * 2, name="results"
    )(*outs)


def shards(tokens, upstream, expert_ids, gate_probs, pad_mask, gate_weight, up_weight, down_weight):
    tok_count, top_count = expert_ids.shape
    experts = lax.axis_size("expert")
    capacity = min(tok_count, 2 * tok_count * top_count // experts)
    if capacity == tok_count and experts > 1 and experts & (experts - 1) == 0:
        return fused(
            tokens, upstream, expert_ids, gate_probs, pad_mask, gate_weight, up_weight, down_weight
        )
    slots_total = experts * capacity
    full_width = tokens.shape[1] * lax.axis_size("half")
    slot_dest = assign_slots(expert_ids, experts, capacity)
    place_items = placement_matrix(slot_dest, slots_total)
    place_tokens = jnp.sum(place_items.reshape(slots_total, tok_count, top_count), axis=2)
    weight_gate = gate_weight[0]
    weight_up = up_weight[0]
    weight_down = down_weight[0]
    rows_in = to_experts(place_tokens, tokens)
    gate_val = jnp.dot(rows_in, weight_gate, preferred_element_type=jnp.float32)
    up_val = jnp.dot(rows_in, weight_up, preferred_element_type=jnp.float32)
    hidden_act = (jax.nn.silu(gate_val) * up_val).astype(jnp.bfloat16)
    partial_value = jnp.dot(hidden_act, weight_down, preferred_element_type=jnp.float32)
    out_home = to_homes(partial_value)
    outputs = jnp.take(out_home, slot_dest, axis=0).reshape(tok_count, top_count, -1)
    out_float = outputs.astype(jnp.float32)
    shares = gate_probs / jnp.sum(gate_probs, axis=1, keepdims=True)
    layer_out = jnp.sum(shares[:, :, None] * out_float, axis=1).astype(jnp.bfloat16)
    gram_part = jnp.einsum("tjd,tkd->tjk", out_float, out_float) / math.sqrt(full_width)
    gram = lax.psum(gram_part, "half")
    off_diag = 1.0 - jnp.eye(top_count, dtype=jnp.float32)
    coeffs = orth_weight * gram * off_diag
    grad_out = pad_mask.astype(jnp.float32)[:, None, None] * (
        shares[:, :, None] * upstream.astype(jnp.float32)[:, None, :]
        + jnp.einsum("tjk,tkd->tjd", coeffs, out_float)
    )
    grad_items = grad_out.astype(jnp.bfloat16).reshape(tok_count * top_count, -1)
    grad_rows = to_experts(place_items, grad_items)
    grad_act = jnp.einsum("rd,hd->rh", grad_rows, weight_down, preferred_element_type=jnp.float32)
    sigma = jax.nn.sigmoid(gate_val)
    grad_gate = (grad_act * up_val * sigma * (1.0 + gate_val * (1.0 - sigma))).astype(jnp.bfloat16)
    grad_up = (grad_act * gate_val * sigma).astype(jnp.bfloat16)
    grad_partial = jnp.einsum(
        "rh,dh->rd", grad_gate, weight_gate, preferred_element_type=jnp.float32
    )
    grad_partial = grad_partial + jnp.einsum(
        "rh,dh->rd", grad_up, weight_up, preferred_element_type=jnp.float32
    )
    grad_home = to_homes(grad_partial)
    grad_pairs = jnp.take(grad_home, slot_dest, axis=0).reshape(tok_count, top_count, -1)
    grad_tokens = jnp.sum(grad_pairs.astype(jnp.float32), axis=1).astype(jnp.bfloat16)
    return (layer_out, grad_tokens)


def solution(mesh):
    in_specs = (
        P("expert", "half"),
        P("expert", "half"),
        P("expert", None),
        P("expert", None),
        P("expert"),
        P("expert", None, "half"),
        P("expert", None, "half"),
        P("expert", "half", None),
    )
    out_specs = (P("expert", "half"), P("expert", "half"))
    return jax.shard_map(shards, mesh=mesh, in_specs=in_specs, out_specs=out_specs, check_vma=False)
```

```python
import functools
import math

import jax
import jax.numpy as jnp
from jax import lax
from jax.experimental import pallas as pl
from jax.experimental.pallas import tpu as pltpu
from jax.sharding import PartitionSpec as P

orth_weight = 0.25


def assign_slots(expert_ids, experts, capacity):
    tok_count, top_count = expert_ids.shape
    flat_ids = expert_ids.reshape(tok_count * top_count)
    onehot = (flat_ids[:, None] == jnp.arange(experts, dtype=jnp.int32)[None, :]).astype(jnp.int32)
    before = jnp.cumsum(onehot, axis=0) - onehot
    slot_index = jnp.sum(before * onehot, axis=1)
    return flat_ids * capacity + slot_index


def placement_matrix(slot_dest, slots_total):
    row_index = jnp.arange(slots_total, dtype=jnp.int32)
    return (row_index[:, None] == slot_dest[None, :]).astype(jnp.bfloat16)


def to_experts(place, items):
    whole = lax.all_gather(items, "half", axis=1, tiled=True)
    buckets = jnp.dot(place, whole, preferred_element_type=jnp.float32).astype(jnp.bfloat16)
    return lax.all_to_all(buckets, "expert", split_axis=0, concat_axis=0, tiled=True)


def to_homes(partial_value):
    summed = lax.psum_scatter(
        partial_value.astype(jnp.bfloat16), "half", scatter_dimension=1, tiled=True
    )
    return lax.all_to_all(summed, "expert", split_axis=0, concat_axis=0, tiled=True)


def block_of(width):
    return next((b for b in (256, 128) if width % b == 0), width)


def tiles(width, body):
    size = block_of(width)

    def step(j, carry):
        body(pl.ds(pl.multiple_of(j * size, size), size), size)
        return carry

    lax.fori_loop(0, width // size, step, 0)


def dot(a, b):
    return jnp.dot(a, b, preferred_element_type=jnp.float32)


def dot_t(a, b):
    return lax.dot_general(a, b, (((1,), (1,)), ((), ())), preferred_element_type=jnp.float32)


def copy_kernel(a_ref, b_ref, a_out, b_out):
    a_out[...] = a_ref[...]
    b_out[...] = b_ref[...]


def fused_kernel(
    n, halves,
    tok_hbm, up_hbm, ids_hbm, probs_hbm, pad_hbm, wg_hbm, wu_hbm, wd_hbm,
    layer_ref, gtok_ref,
    up_ref, ids_ref, probs_ref, pad_ref,
    tok_buf, wg, wu, wd, gate_v, up_v, act_v, hid, gg, gu,
    osend, orecv, ored, xrecv, xs, gram_s, whole_s, gsend, grows, psend, prec, fsend, frecv, rsend, fin,
    w_sem, tok_ss, tok_rs, part_ss, part_rs, out_ss, out_rs, gram_ss, gram_rs,
    grad_ss, grad_rs, relay_ss, pair_ss, pair_rs, fpart_ss, fpart_rs, fin_ss, fin_rs,
):
    e = lax.axis_index("expert")
    h = lax.axis_index("half")
    tok, width = up_ref.shape
    hidden = wg.shape[1]
    rows = n * tok
    chips = n // 2
    group = min(n, 8)
    parity = lax.rem(e, 2)
    chip = lax.div(e, 2)
    sibling = e + 1 - 2 * parity
    full = halves * width

    def remote(src, dst, ssem, rsem, pe, ph):
        return pltpu.make_async_remote_copy(
            src_ref=src, dst_ref=dst, send_sem=ssem, recv_sem=rsem,
            device_id=(pe, ph), device_id_type=pl.DeviceIdType.MESH,
        )

    def wrap(a, d, size):
        return lax.rem(a + d, size)

    def flip(a, d):
        bit = 1
        out = a
        while bit <= d:
            if d & bit:
                out = out + bit * (1 - 2 * lax.rem(lax.div(a, bit), 2))
            bit *= 2
        return out

    def arrived(slot, rsem):
        remote(slot, slot, pair_ss.at[0], rsem, sibling, h).wait_recv()

    sends = []

    def send(*args):
        c = remote(*args)
        c.start()
        sends.append(c)

    moves = (
        (tok_hbm, tok_buf.at[h, e]), (ids_hbm, ids_ref), (probs_hbm, probs_ref),
        (pad_hbm, pad_ref), (up_hbm, up_ref),
        (wg_hbm.at[0], wg), (wu_hbm.at[0], wu), (wd_hbm.at[0], wd),
    )
    loads = [pltpu.make_async_copy(src, dst, w_sem.at[i]) for i, (src, dst) in enumerate(moves)]
    for c in loads:
        c.start()

    others = list(range(1, halves))
    near = list(range(1, n))
    outer = near[::-1]
    chips_near = list(range(1, chips))
    chips_far = chips_near[::-1]

    barrier = pltpu.get_barrier_semaphore()
    for d in outer:
        pl.semaphore_signal(
            barrier, inc=1, device_id=(flip(e, d), h), device_id_type=pl.DeviceIdType.MESH
        )
    for d in others:
        pl.semaphore_signal(
            barrier, inc=1, device_id=(e, wrap(h, d, halves)), device_id_type=pl.DeviceIdType.MESH
        )
    pl.semaphore_wait(barrier, len(outer) + len(others))

    loads[0].wait()
    k = 0
    mine = tok_buf.at[h, e]
    for d in [d for d in chips_far if d % 2 == 0 or d == 1]:
        send(mine, mine, tok_ss.at[k], tok_rs.at[h, e], 2 * flip(chip, d) + parity, h)
        k += 1
    for d in others:
        send(mine, mine, tok_ss.at[k], tok_rs.at[h, e], e, wrap(h, d, halves))
        k += 1
    send(mine, mine, tok_ss.at[k], tok_rs.at[h, e], sibling, h)
    k += 1
    coming = sorted(chips_near, key=lambda d: (d // 4, d % 2, d))
    for d in coming:
        pe = 2 * flip(chip, d) + parity
        slot = tok_buf.at[h, pe]
        arrived(slot, tok_rs.at[h, pe])
        if d % 2 == 0:
            beside = 2 * flip(chip, 1) + parity
            send(slot, slot, tok_ss.at[k], tok_rs.at[h, pe], beside, h)
            k += 1
        for dh in others:
            send(slot, slot, tok_ss.at[k], tok_rs.at[h, pe], e, wrap(h, dh, halves))
            k += 1
        send(slot, slot, tok_ss.at[k], tok_rs.at[h, pe], sibling, h)
        k += 1
    for d in [0] + coming:
        pe = 2 * flip(chip, d) + parity
        for dh in others:
            ph = wrap(h, halves - dh, halves)
            slot = tok_buf.at[ph, pe]
            arrived(slot, tok_rs.at[ph, pe])
            send(slot, slot, tok_ss.at[k], tok_rs.at[ph, pe], sibling, h)
            k += 1
    for c in loads[1:7]:
        c.wait()
    for dh in [0] + others:
        ph = wrap(h, halves - dh, halves)
        for d in [0] + coming:
            pe = 2 * flip(chip, d) + 1 - parity
            arrived(tok_buf.at[ph, pe], tok_rs.at[ph, pe])

        def hidden_step(cols, size, ph=ph, dh=dh):
            at = pl.ds(pl.multiple_of(ph * width, width), width)
            x = tok_buf[ph].reshape(rows, width)
            gate = dot(x, wg[at, cols])
            up = dot(x, wu[at, cols])
            if dh:
                gate = gate + gate_v[:, cols]
                up = up + up_v[:, cols]
            gate_v[:, cols] = gate
            up_v[:, cols] = up
            if dh == halves - 1:
                hid[:, cols] = (gate / (1.0 + jnp.exp(-gate)) * up).astype(jnp.bfloat16)

        tiles(hidden, hidden_step)
    loads[7].wait()

    for dh in others + [0]:
        ph = wrap(h, dh, halves)

        def down_step(cols, size, ph=ph, dh=dh):
            at = pl.ds(pl.multiple_of(cols.start + ph * width, size), size)
            part = dot(hid[...], wd[:, at])
            osend[dh, :, :, cols] = part.reshape(n, tok, size).astype(jnp.bfloat16)

        tiles(width, down_step)
        if dh:
            for j, d in enumerate(outer + [0]):
                pe = flip(e, d)
                send(
                    osend.at[dh, pe], orecv.at[halves - dh, pe],
                    part_ss.at[dh, j], part_rs.at[halves - dh, j], e, ph,
                )

    eye = (
        lax.broadcasted_iota(jnp.int32, (tok, tok), 0)
        == lax.broadcasted_iota(jnp.int32, (tok, tok), 1)
    )
    top = ids_ref.shape[0]
    lane = lax.broadcasted_iota(jnp.int32, (tok, top), 1)

    def column(row):
        return jnp.sum(jnp.where(eye, jnp.broadcast_to(row, (tok, tok)), 0.0), axis=1, keepdims=True)

    ids = jnp.zeros((tok, top), jnp.float32)
    probs = jnp.zeros((tok, top), jnp.float32)
    for j in range(top):
        ids = jnp.where(lane == j, column(ids_ref[j:j + 1, :].astype(jnp.float32)), ids)
        probs = jnp.where(lane == j, column(probs_ref[j:j + 1, :]), probs)
    pad = column(pad_ref[...].astype(jnp.float32))
    shares = probs / jnp.sum(probs, axis=1, keepdims=True)
    for j, d in enumerate(outer + [0]):
        pe = flip(e, d)
        total = osend[0, pe].astype(jnp.float32)
        for dh in others:
            arrived(orecv.at[dh, pe], part_rs.at[dh, j])
            total = total + orecv[dh, pe].astype(jnp.float32)
        if d:
            ored[pe] = total.astype(jnp.bfloat16)
            send(ored.at[pe], xrecv.at[e], out_ss.at[j], out_rs.at[e], pe, h)
        else:
            xrecv[e] = total.astype(jnp.bfloat16)
    def share_of(i):
        listed = (ids == i.astype(jnp.float32)).astype(jnp.float32)
        return jnp.sum(listed * shares, axis=1, keepdims=True), jnp.sum(listed, axis=1, keepdims=True)

    layer = jnp.zeros((tok, width), jnp.float32)
    for d in [0] + near:
        pe = flip(e, d)
        share, listed = share_of(pe)
        if d:
            arrived(xrecv.at[pe], out_rs.at[pe])
        value = jnp.where(listed > 0.0, xrecv[pe].astype(jnp.float32), 0.0)
        xs[pe] = value.astype(jnp.bfloat16)
        layer = layer + share * value

    x_all = xs[...].reshape(rows, width)
    same = (
        lax.rem(lax.broadcasted_iota(jnp.int32, (tok, rows), 1), tok)
        == lax.broadcasted_iota(jnp.int32, (tok, rows), 0)
    ).astype(jnp.float32)
    gram = dot_t(x_all, x_all).reshape(n, tok, rows) * same[None]
    gram_s[h] = jnp.sum(gram, axis=1)
    for dh in range(1, halves):
        send(gram_s.at[h], gram_s.at[h], gram_ss.at[dh], gram_rs.at[h], e, wrap(h, dh, halves))
    for dh in range(1, halves):
        ph = wrap(h, halves - dh, halves)
        arrived(gram_s.at[ph], gram_rs.at[ph])
    whole = gram_s[0]
    for i in range(1, halves):
        whole = whole + gram_s[i]
    apart = (
        lax.div(lax.broadcasted_iota(jnp.int32, (n, rows), 1), tok)
        != lax.broadcasted_iota(jnp.int32, (n, rows), 0)
    ).astype(jnp.float32)
    whole = whole * (apart * (orth_weight / math.sqrt(full)))
    whole_s[...] = whole
    x_all = xs[...].reshape(rows, width)
    upstream = up_ref[...].astype(jnp.float32)
    for g in range(n // group):
        first = pl.multiple_of(flip(lax.div(e, group), g) * group, group)
        coeffs = whole_s[pl.ds(first, group), :][:, None, :] * same[None]
        coeffs = coeffs.reshape(group * tok, rows)
        high = coeffs.astype(jnp.bfloat16)
        low = (coeffs - high.astype(jnp.float32)).astype(jnp.bfloat16)
        mixed = (dot(high, x_all) + dot(low, x_all)).reshape(group, tok, width)
        for i in range(group):
            share, _ = share_of(first + i)
            gsend[first + i] = (pad * (share * upstream + mixed[i])).astype(jnp.bfloat16)
        for d in range(max(1, g * group), (g + 1) * group):
            pe = flip(e, d)
            send(gsend.at[pe], grows.at[h, e], grad_ss.at[d], grad_rs.at[h, e], pe, h)
        if g == 0:
            for dh in others:
                send(
                    gsend.at[e], grows.at[h, e], relay_ss.at[dh - 1], grad_rs.at[h, e],
                    e, wrap(h, dh, halves),
                )
    layer_ref[...] = layer.astype(jnp.bfloat16)
    k = len(others)
    grows[h, e] = gsend[e]
    for d in near:
        pe = flip(e, d)
        slot = grows.at[h, pe]
        arrived(slot, grad_rs.at[h, pe])
        for dh in others:
            send(slot, slot, relay_ss.at[k], grad_rs.at[h, pe], e, wrap(h, dh, halves))
            k += 1
    for dh in [0] + others:
        ph = wrap(h, halves - dh, halves)
        if dh:
            for d in [0] + near:
                pe = flip(e, d)
                arrived(grows.at[ph, pe], grad_rs.at[ph, pe])

        def act_step(cols, size, ph=ph, dh=dh):
            at = pl.ds(pl.multiple_of(ph * width, width), width)
            act = dot_t(grows[ph].reshape(rows, width), wd[cols, at])
            if dh:
                act = act + act_v[:, cols]
            if dh < halves - 1:
                act_v[:, cols] = act
            else:
                gate = gate_v[:, cols]
                sigma = 1.0 / (1.0 + jnp.exp(-gate))
                gg[:, cols] = (
                    act * up_v[:, cols] * sigma * (1.0 + gate * (1.0 - sigma))
                ).astype(jnp.bfloat16)
                gu[:, cols] = (act * gate * sigma).astype(jnp.bfloat16)

        tiles(hidden, act_step)

    for dh in others + [0]:
        ph = wrap(h, dh, halves)

        def back_step(cols, size, ph=ph, dh=dh):
            at = pl.ds(pl.multiple_of(cols.start + ph * width, size), size)
            part = dot_t(gg[...], wg[at, :]) + dot_t(gu[...], wu[at, :])
            part = part.astype(jnp.bfloat16).reshape(chips, 2, tok, size)
            for q in range(2):
                psend[dh, q, :, :, cols] = part[:, q]

        tiles(width, back_step)
        send(psend.at[dh, 1 - parity], prec.at[dh], pair_ss.at[dh], pair_rs.at[dh], sibling, h)
    order = chips_far + [0]
    for dh in others:
        arrived(prec.at[dh], pair_rs.at[dh])
        for j, d in enumerate(order):
            pm = flip(chip, d)
            fsend[dh, pm] = (
                psend[dh, parity, pm].astype(jnp.float32) + prec[dh, pm].astype(jnp.float32)
            ).astype(jnp.bfloat16)
            send(
                fsend.at[dh, pm], frecv.at[halves - dh, pm],
                fpart_ss.at[dh, j], fpart_rs.at[halves - dh, j], e, wrap(h, dh, halves),
            )
    arrived(prec.at[0], pair_rs.at[0])
    for j, d in enumerate(order):
        pm = flip(chip, d)
        total = psend[0, parity, pm].astype(jnp.float32) + prec[0, pm].astype(jnp.float32)
        for dh in others:
            arrived(frecv.at[dh, pm], fpart_rs.at[dh, j])
            total = total + frecv[dh, pm].astype(jnp.float32)
        if d:
            rsend[pm] = total.astype(jnp.bfloat16)
            send(rsend.at[pm], fin.at[chip], fin_ss.at[j], fin_rs.at[chip], 2 * pm + parity, h)
    for d in chips_near:
        pm = flip(chip, d)
        arrived(fin.at[pm], fin_rs.at[pm])
        total = total + fin[pm].astype(jnp.float32)
    gtok_ref[...] = total.astype(jnp.bfloat16)
    for c in sends:
        c.wait_send()


def fused(tokens, upstream, expert_ids, gate_probs, pad_mask, gate_weight, up_weight, down_weight):
    n, halves = lax.axis_size("expert"), lax.axis_size("half")
    tok, width = tokens.shape
    hidden = gate_weight.shape[2]
    rows, full, chips = n * tok, halves * width, n // 2
    top = expert_ids.shape[1]
    low, wide = jnp.bfloat16, jnp.float32
    vmem, dma = pltpu.VMEM, pltpu.SemaphoreType.DMA
    local = pl.BlockSpec(memory_space=pltpu.VMEM)
    remain = pl.BlockSpec(memory_space=pl.ANY)
    result = [jax.ShapeDtypeStruct((tok, width), low)] * 2
    outs = pl.pallas_call(
        functools.partial(fused_kernel, n, halves),
        out_shape=result,
        in_specs=[remain] * 8,
        out_specs=[local] * 2,
        scratch_shapes=[
            vmem((tok, width), low),
            vmem((top, tok), jnp.int32),
            vmem((top, tok), wide),
            vmem((1, tok), jnp.int32),
            vmem((halves, n, tok, width), low),
            vmem((full, hidden), low),
            vmem((full, hidden), low),
            vmem((hidden, full), low),
            vmem((rows, hidden), wide),
            vmem((rows, hidden), wide),
            vmem((rows, hidden), wide),
            vmem((rows, hidden), low),
            vmem((rows, hidden), low),
            vmem((rows, hidden), low),
            vmem((halves, n, tok, width), low),
            vmem((halves, n, tok, width), low),
            vmem((n, tok, width), low),
            vmem((n, tok, width), low),
            vmem((n, tok, width), low),
            vmem((halves, n, rows), wide),
            vmem((n, rows), wide),
            vmem((n, tok, width), low),
            vmem((halves, n, tok, width), low),
            vmem((halves, 2, chips, tok, width), low),
            vmem((halves, chips, tok, width), low),
            vmem((halves, chips, tok, width), low),
            vmem((halves, chips, tok, width), low),
            vmem((chips, tok, width), low),
            vmem((chips, tok, width), low),
            dma((8,)),
            dma((2 * halves * n,)),
            dma((halves, n)),
            dma((halves, n)),
            dma((halves, n)),
            dma((n,)),
            dma((n,)),
            dma((halves,)),
            dma((halves,)),
            dma((n,)),
            dma((halves, n)),
            dma((halves * n,)),
            dma((halves,)),
            dma((halves,)),
            dma((halves, chips)),
            dma((halves, chips)),
            dma((chips,)),
            dma((chips,)),
        ],
        compiler_params=pltpu.CompilerParams(
            collective_id=0, has_side_effects=True, vmem_limit_bytes=56 * 1024 * 1024
        ),
        name="experts",
    )(
        tokens, upstream, expert_ids.T, gate_probs.T, pad_mask.reshape(1, tok),
        gate_weight, up_weight, down_weight,
    )
    return pl.pallas_call(
        copy_kernel, out_shape=result, in_specs=[local] * 2, out_specs=[local] * 2, name="results"
    )(*outs)


def shards(tokens, upstream, expert_ids, gate_probs, pad_mask, gate_weight, up_weight, down_weight):
    tok_count, top_count = expert_ids.shape
    experts = lax.axis_size("expert")
    capacity = min(tok_count, 2 * tok_count * top_count // experts)
    if capacity == tok_count and experts > 1 and experts & (experts - 1) == 0:
        return fused(
            tokens, upstream, expert_ids, gate_probs, pad_mask, gate_weight, up_weight, down_weight
        )
    slots_total = experts * capacity
    full_width = tokens.shape[1] * lax.axis_size("half")
    slot_dest = assign_slots(expert_ids, experts, capacity)
    place_items = placement_matrix(slot_dest, slots_total)
    place_tokens = jnp.sum(place_items.reshape(slots_total, tok_count, top_count), axis=2)
    weight_gate = gate_weight[0]
    weight_up = up_weight[0]
    weight_down = down_weight[0]
    rows_in = to_experts(place_tokens, tokens)
    gate_val = jnp.dot(rows_in, weight_gate, preferred_element_type=jnp.float32)
    up_val = jnp.dot(rows_in, weight_up, preferred_element_type=jnp.float32)
    hidden_act = (jax.nn.silu(gate_val) * up_val).astype(jnp.bfloat16)
    partial_value = jnp.dot(hidden_act, weight_down, preferred_element_type=jnp.float32)
    out_home = to_homes(partial_value)
    outputs = jnp.take(out_home, slot_dest, axis=0).reshape(tok_count, top_count, -1)
    out_float = outputs.astype(jnp.float32)
    shares = gate_probs / jnp.sum(gate_probs, axis=1, keepdims=True)
    layer_out = jnp.sum(shares[:, :, None] * out_float, axis=1).astype(jnp.bfloat16)
    gram_part = jnp.einsum("tjd,tkd->tjk", out_float, out_float) / math.sqrt(full_width)
    gram = lax.psum(gram_part, "half")
    off_diag = 1.0 - jnp.eye(top_count, dtype=jnp.float32)
    coeffs = orth_weight * gram * off_diag
    grad_out = pad_mask.astype(jnp.float32)[:, None, None] * (
        shares[:, :, None] * upstream.astype(jnp.float32)[:, None, :]
        + jnp.einsum("tjk,tkd->tjd", coeffs, out_float)
    )
    grad_items = grad_out.astype(jnp.bfloat16).reshape(tok_count * top_count, -1)
    grad_rows = to_experts(place_items, grad_items)
    grad_act = jnp.einsum("rd,hd->rh", grad_rows, weight_down, preferred_element_type=jnp.float32)
    sigma = jax.nn.sigmoid(gate_val)
    grad_gate = (grad_act * up_val * sigma * (1.0 + gate_val * (1.0 - sigma))).astype(jnp.bfloat16)
    grad_up = (grad_act * gate_val * sigma).astype(jnp.bfloat16)
    grad_partial = jnp.einsum(
        "rh,dh->rd", grad_gate, weight_gate, preferred_element_type=jnp.float32
    )
    grad_partial = grad_partial + jnp.einsum(
        "rh,dh->rd", grad_up, weight_up, preferred_element_type=jnp.float32
    )
    grad_home = to_homes(grad_partial)
    grad_pairs = jnp.take(grad_home, slot_dest, axis=0).reshape(tok_count, top_count, -1)
    grad_tokens = jnp.sum(grad_pairs.astype(jnp.float32), axis=1).astype(jnp.bfloat16)
    return (layer_out, grad_tokens)


def solution(mesh):
    in_specs = (
        P("expert", "half"),
        P("expert", "half"),
        P("expert", None),
        P("expert", None),
        P("expert"),
        P("expert", None, "half"),
        P("expert", None, "half"),
        P("expert", "half", None),
    )
    out_specs = (P("expert", "half"), P("expert", "half"))
    return jax.shard_map(shards, mesh=mesh, in_specs=in_specs, out_specs=out_specs, check_vma=False)
```

```python
import functools
import math

import jax
import jax.numpy as jnp
from jax import lax
from jax.experimental import pallas as pl
from jax.experimental.pallas import tpu as pltpu
from jax.sharding import PartitionSpec as P

orth_weight = 0.25


def assign_slots(expert_ids, experts, capacity):
    tok_count, top_count = expert_ids.shape
    flat_ids = expert_ids.reshape(tok_count * top_count)
    onehot = (flat_ids[:, None] == jnp.arange(experts, dtype=jnp.int32)[None, :]).astype(jnp.int32)
    before = jnp.cumsum(onehot, axis=0) - onehot
    slot_index = jnp.sum(before * onehot, axis=1)
    return flat_ids * capacity + slot_index


def placement_matrix(slot_dest, slots_total):
    row_index = jnp.arange(slots_total, dtype=jnp.int32)
    return (row_index[:, None] == slot_dest[None, :]).astype(jnp.bfloat16)


def to_experts(place, items):
    whole = lax.all_gather(items, "half", axis=1, tiled=True)
    buckets = jnp.dot(place, whole, preferred_element_type=jnp.float32).astype(jnp.bfloat16)
    return lax.all_to_all(buckets, "expert", split_axis=0, concat_axis=0, tiled=True)


def to_homes(partial_value):
    summed = lax.psum_scatter(
        partial_value.astype(jnp.bfloat16), "half", scatter_dimension=1, tiled=True
    )
    return lax.all_to_all(summed, "expert", split_axis=0, concat_axis=0, tiled=True)


def block_of(width):
    return next((b for b in (256, 128) if width % b == 0), width)


def tiles(width, body):
    size = block_of(width)

    def step(j, carry):
        body(pl.ds(pl.multiple_of(j * size, size), size), size)
        return carry

    lax.fori_loop(0, width // size, step, 0)


def dot(a, b):
    return jnp.dot(a, b, preferred_element_type=jnp.float32)


def dot_t(a, b):
    return lax.dot_general(a, b, (((1,), (1,)), ((), ())), preferred_element_type=jnp.float32)


def copy_kernel(a_ref, b_ref, a_out, b_out):
    a_out[...] = a_ref[...]
    b_out[...] = b_ref[...]


def fused_kernel(
    n, halves,
    tok_hbm, up_hbm, ids_hbm, probs_hbm, pad_hbm, wg_hbm, wu_hbm, wd_hbm,
    layer_ref, gtok_ref,
    up_ref, ids_ref, probs_ref, pad_ref,
    tok_buf, wg, wu, wd, gate_v, up_v, act_v, hid, gg, gu,
    osend, orecv, ored, xrecv, xs, gram_s, whole_s, gsend, grows, psend, prec, fsend, frecv, rsend, fin,
    w_sem, tok_ss, tok_rs, part_ss, part_rs, out_ss, out_rs, gram_ss, gram_rs,
    grad_ss, grad_rs, relay_ss, pair_ss, pair_rs, fpart_ss, fpart_rs, fin_ss, fin_rs,
):
    e = lax.axis_index("expert")
    h = lax.axis_index("half")
    tok, width = up_ref.shape
    hidden = wg.shape[1]
    rows = n * tok
    chips = n // 2
    group = min(n, 8)
    parity = lax.rem(e, 2)
    chip = lax.div(e, 2)
    sibling = e + 1 - 2 * parity
    full = halves * width

    def remote(src, dst, ssem, rsem, pe, ph):
        return pltpu.make_async_remote_copy(
            src_ref=src, dst_ref=dst, send_sem=ssem, recv_sem=rsem,
            device_id=(pe, ph), device_id_type=pl.DeviceIdType.MESH,
        )

    def wrap(a, d, size):
        return lax.rem(a + d, size)

    def flip(a, d):
        bit = 1
        out = a
        while bit <= d:
            if d & bit:
                out = out + bit * (1 - 2 * lax.rem(lax.div(a, bit), 2))
            bit *= 2
        return out

    def arrived(slot, rsem):
        remote(slot, slot, pair_ss.at[0], rsem, sibling, h).wait_recv()

    sends = []

    def send(*args):
        c = remote(*args)
        c.start()
        sends.append(c)

    moves = (
        (tok_hbm, tok_buf.at[h, e]), (ids_hbm, ids_ref), (probs_hbm, probs_ref),
        (pad_hbm, pad_ref), (up_hbm, up_ref),
        (wg_hbm.at[0], wg), (wu_hbm.at[0], wu), (wd_hbm.at[0], wd),
    )
    loads = [pltpu.make_async_copy(src, dst, w_sem.at[i]) for i, (src, dst) in enumerate(moves)]
    for c in loads:
        c.start()

    others = list(range(1, halves))
    near = list(range(1, n))
    outer = near[::-1]
    chips_near = list(range(1, chips))
    chips_far = chips_near[::-1]

    barrier = pltpu.get_barrier_semaphore()
    for d in outer:
        pl.semaphore_signal(
            barrier, inc=1, device_id=(flip(e, d), h), device_id_type=pl.DeviceIdType.MESH
        )
    for d in others:
        pl.semaphore_signal(
            barrier, inc=1, device_id=(e, wrap(h, d, halves)), device_id_type=pl.DeviceIdType.MESH
        )
    pl.semaphore_wait(barrier, len(outer) + len(others))

    loads[0].wait()
    k = 0
    mine = tok_buf.at[h, e]
    for d in chips_far:
        send(mine, mine, tok_ss.at[k], tok_rs.at[h, e], 2 * flip(chip, d) + parity, h)
        k += 1
    for d in others:
        send(mine, mine, tok_ss.at[k], tok_rs.at[h, e], e, wrap(h, d, halves))
        k += 1
    send(mine, mine, tok_ss.at[k], tok_rs.at[h, e], sibling, h)
    k += 1
    for d in chips_near:
        pe = 2 * flip(chip, d) + parity
        slot = tok_buf.at[h, pe]
        arrived(slot, tok_rs.at[h, pe])
        for dh in others:
            send(slot, slot, tok_ss.at[k], tok_rs.at[h, pe], e, wrap(h, dh, halves))
            k += 1
        send(slot, slot, tok_ss.at[k], tok_rs.at[h, pe], sibling, h)
        k += 1
    for d in [0] + chips_near:
        pe = 2 * flip(chip, d) + parity
        for dh in others:
            ph = wrap(h, halves - dh, halves)
            slot = tok_buf.at[ph, pe]
            arrived(slot, tok_rs.at[ph, pe])
            send(slot, slot, tok_ss.at[k], tok_rs.at[ph, pe], sibling, h)
            k += 1
    for c in loads[1:7]:
        c.wait()
    for dh in [0] + others:
        ph = wrap(h, halves - dh, halves)
        for d in [0] + chips_near:
            pe = 2 * flip(chip, d) + 1 - parity
            arrived(tok_buf.at[ph, pe], tok_rs.at[ph, pe])

        def hidden_step(cols, size, ph=ph, dh=dh):
            at = pl.ds(pl.multiple_of(ph * width, width), width)
            x = tok_buf[ph].reshape(rows, width)
            gate = dot(x, wg[at, cols])
            up = dot(x, wu[at, cols])
            if dh:
                gate = gate + gate_v[:, cols]
                up = up + up_v[:, cols]
            gate_v[:, cols] = gate
            up_v[:, cols] = up
            if dh == halves - 1:
                hid[:, cols] = (gate / (1.0 + jnp.exp(-gate)) * up).astype(jnp.bfloat16)

        tiles(hidden, hidden_step)
    loads[7].wait()

    for dh in others + [0]:
        ph = wrap(h, dh, halves)

        def down_step(cols, size, ph=ph, dh=dh):
            at = pl.ds(pl.multiple_of(cols.start + ph * width, size), size)
            part = dot(hid[...], wd[:, at])
            osend[dh, :, :, cols] = part.reshape(n, tok, size).astype(jnp.bfloat16)

        tiles(width, down_step)
        if dh:
            for j, d in enumerate(outer + [0]):
                pe = flip(e, d)
                send(
                    osend.at[dh, pe], orecv.at[halves - dh, pe],
                    part_ss.at[dh, j], part_rs.at[halves - dh, j], e, ph,
                )

    eye = (
        lax.broadcasted_iota(jnp.int32, (tok, tok), 0)
        == lax.broadcasted_iota(jnp.int32, (tok, tok), 1)
    )
    top = ids_ref.shape[0]
    lane = lax.broadcasted_iota(jnp.int32, (tok, top), 1)

    def column(row):
        return jnp.sum(jnp.where(eye, jnp.broadcast_to(row, (tok, tok)), 0.0), axis=1, keepdims=True)

    ids = jnp.zeros((tok, top), jnp.float32)
    probs = jnp.zeros((tok, top), jnp.float32)
    for j in range(top):
        ids = jnp.where(lane == j, column(ids_ref[j:j + 1, :].astype(jnp.float32)), ids)
        probs = jnp.where(lane == j, column(probs_ref[j:j + 1, :]), probs)
    pad = column(pad_ref[...].astype(jnp.float32))
    shares = probs / jnp.sum(probs, axis=1, keepdims=True)
    for j, d in enumerate(outer + [0]):
        pe = flip(e, d)
        total = osend[0, pe].astype(jnp.float32)
        for dh in others:
            arrived(orecv.at[dh, pe], part_rs.at[dh, j])
            total = total + orecv[dh, pe].astype(jnp.float32)
        if d:
            ored[pe] = total.astype(jnp.bfloat16)
            send(ored.at[pe], xrecv.at[e], out_ss.at[j], out_rs.at[e], pe, h)
        else:
            xrecv[e] = total.astype(jnp.bfloat16)
    def share_of(i):
        listed = (ids == i.astype(jnp.float32)).astype(jnp.float32)
        return jnp.sum(listed * shares, axis=1, keepdims=True), jnp.sum(listed, axis=1, keepdims=True)

    layer = jnp.zeros((tok, width), jnp.float32)
    for d in [0] + near:
        pe = flip(e, d)
        share, listed = share_of(pe)
        if d:
            arrived(xrecv.at[pe], out_rs.at[pe])
        value = jnp.where(listed > 0.0, xrecv[pe].astype(jnp.float32), 0.0)
        xs[pe] = value.astype(jnp.bfloat16)
        layer = layer + share * value

    x_all = xs[...].reshape(rows, width)
    same = (
        lax.rem(lax.broadcasted_iota(jnp.int32, (tok, rows), 1), tok)
        == lax.broadcasted_iota(jnp.int32, (tok, rows), 0)
    ).astype(jnp.float32)
    gram = dot_t(x_all, x_all).reshape(n, tok, rows) * same[None]
    gram_s[h] = jnp.sum(gram, axis=1)
    for dh in range(1, halves):
        send(gram_s.at[h], gram_s.at[h], gram_ss.at[dh], gram_rs.at[h], e, wrap(h, dh, halves))
    for dh in range(1, halves):
        ph = wrap(h, halves - dh, halves)
        arrived(gram_s.at[ph], gram_rs.at[ph])
    whole = gram_s[0]
    for i in range(1, halves):
        whole = whole + gram_s[i]
    apart = (
        lax.div(lax.broadcasted_iota(jnp.int32, (n, rows), 1), tok)
        != lax.broadcasted_iota(jnp.int32, (n, rows), 0)
    ).astype(jnp.float32)
    whole = whole * (apart * (orth_weight / math.sqrt(full)))
    whole_s[...] = whole
    x_all = xs[...].reshape(rows, width)
    upstream = up_ref[...].astype(jnp.float32)
    for g in range(n // group):
        first = pl.multiple_of(flip(lax.div(e, group), g) * group, group)
        coeffs = whole_s[pl.ds(first, group), :][:, None, :] * same[None]
        coeffs = coeffs.reshape(group * tok, rows)
        high = coeffs.astype(jnp.bfloat16)
        low = (coeffs - high.astype(jnp.float32)).astype(jnp.bfloat16)
        mixed = (dot(high, x_all) + dot(low, x_all)).reshape(group, tok, width)
        for i in range(group):
            share, _ = share_of(first + i)
            gsend[first + i] = (pad * (share * upstream + mixed[i])).astype(jnp.bfloat16)
        for d in range(max(1, g * group), (g + 1) * group):
            pe = flip(e, d)
            send(gsend.at[pe], grows.at[h, e], grad_ss.at[d], grad_rs.at[h, e], pe, h)
        if g == 0:
            for dh in others:
                send(
                    gsend.at[e], grows.at[h, e], relay_ss.at[dh - 1], grad_rs.at[h, e],
                    e, wrap(h, dh, halves),
                )
    layer_ref[...] = layer.astype(jnp.bfloat16)
    k = len(others)
    grows[h, e] = gsend[e]
    for d in near:
        pe = flip(e, d)
        slot = grows.at[h, pe]
        arrived(slot, grad_rs.at[h, pe])
        for dh in others:
            send(slot, slot, relay_ss.at[k], grad_rs.at[h, pe], e, wrap(h, dh, halves))
            k += 1
    for dh in [0] + others:
        ph = wrap(h, halves - dh, halves)
        if dh:
            for d in [0] + near:
                pe = flip(e, d)
                arrived(grows.at[ph, pe], grad_rs.at[ph, pe])

        def act_step(cols, size, ph=ph, dh=dh):
            at = pl.ds(pl.multiple_of(ph * width, width), width)
            act = dot_t(grows[ph].reshape(rows, width), wd[cols, at])
            if dh:
                act = act + act_v[:, cols]
            if dh < halves - 1:
                act_v[:, cols] = act
            else:
                gate = gate_v[:, cols]
                sigma = 1.0 / (1.0 + jnp.exp(-gate))
                gg[:, cols] = (
                    act * up_v[:, cols] * sigma * (1.0 + gate * (1.0 - sigma))
                ).astype(jnp.bfloat16)
                gu[:, cols] = (act * gate * sigma).astype(jnp.bfloat16)

        tiles(hidden, act_step)

    for dh in others + [0]:
        ph = wrap(h, dh, halves)

        def back_step(cols, size, ph=ph, dh=dh):
            at = pl.ds(pl.multiple_of(cols.start + ph * width, size), size)
            part = dot_t(gg[...], wg[at, :]) + dot_t(gu[...], wu[at, :])
            part = part.astype(jnp.bfloat16).reshape(chips, 2, tok, size)
            for q in range(2):
                psend[dh, q, :, :, cols] = part[:, q]

        tiles(width, back_step)
        send(psend.at[dh, 1 - parity], prec.at[dh], pair_ss.at[dh], pair_rs.at[dh], sibling, h)
    order = chips_far + [0]
    for dh in others:
        arrived(prec.at[dh], pair_rs.at[dh])
        for j, d in enumerate(order):
            pm = flip(chip, d)
            fsend[dh, pm] = (
                psend[dh, parity, pm].astype(jnp.float32) + prec[dh, pm].astype(jnp.float32)
            ).astype(jnp.bfloat16)
            send(
                fsend.at[dh, pm], frecv.at[halves - dh, pm],
                fpart_ss.at[dh, j], fpart_rs.at[halves - dh, j], e, wrap(h, dh, halves),
            )
    arrived(prec.at[0], pair_rs.at[0])
    for j, d in enumerate(order):
        pm = flip(chip, d)
        total = psend[0, parity, pm].astype(jnp.float32) + prec[0, pm].astype(jnp.float32)
        for dh in others:
            arrived(frecv.at[dh, pm], fpart_rs.at[dh, j])
            total = total + frecv[dh, pm].astype(jnp.float32)
        if d:
            rsend[pm] = total.astype(jnp.bfloat16)
            send(rsend.at[pm], fin.at[chip], fin_ss.at[j], fin_rs.at[chip], 2 * pm + parity, h)
    for d in chips_near:
        pm = flip(chip, d)
        arrived(fin.at[pm], fin_rs.at[pm])
        total = total + fin[pm].astype(jnp.float32)
    gtok_ref[...] = total.astype(jnp.bfloat16)
    for c in sends:
        c.wait_send()


def fused(tokens, upstream, expert_ids, gate_probs, pad_mask, gate_weight, up_weight, down_weight):
    n, halves = lax.axis_size("expert"), lax.axis_size("half")
    tok, width = tokens.shape
    hidden = gate_weight.shape[2]
    rows, full, chips = n * tok, halves * width, n // 2
    top = expert_ids.shape[1]
    low, wide = jnp.bfloat16, jnp.float32
    vmem, dma = pltpu.VMEM, pltpu.SemaphoreType.DMA
    local = pl.BlockSpec(memory_space=pltpu.VMEM)
    remain = pl.BlockSpec(memory_space=pl.ANY)
    result = [jax.ShapeDtypeStruct((tok, width), low)] * 2
    outs = pl.pallas_call(
        functools.partial(fused_kernel, n, halves),
        out_shape=result,
        in_specs=[remain] * 8,
        out_specs=[local] * 2,
        scratch_shapes=[
            vmem((tok, width), low),
            vmem((top, tok), jnp.int32),
            vmem((top, tok), wide),
            vmem((1, tok), jnp.int32),
            vmem((halves, n, tok, width), low),
            vmem((full, hidden), low),
            vmem((full, hidden), low),
            vmem((hidden, full), low),
            vmem((rows, hidden), wide),
            vmem((rows, hidden), wide),
            vmem((rows, hidden), wide),
            vmem((rows, hidden), low),
            vmem((rows, hidden), low),
            vmem((rows, hidden), low),
            vmem((halves, n, tok, width), low),
            vmem((halves, n, tok, width), low),
            vmem((n, tok, width), low),
            vmem((n, tok, width), low),
            vmem((n, tok, width), low),
            vmem((halves, n, rows), wide),
            vmem((n, rows), wide),
            vmem((n, tok, width), low),
            vmem((halves, n, tok, width), low),
            vmem((halves, 2, chips, tok, width), low),
            vmem((halves, chips, tok, width), low),
            vmem((halves, chips, tok, width), low),
            vmem((halves, chips, tok, width), low),
            vmem((chips, tok, width), low),
            vmem((chips, tok, width), low),
            dma((8,)),
            dma((2 * halves * n,)),
            dma((halves, n)),
            dma((halves, n)),
            dma((halves, n)),
            dma((n,)),
            dma((n,)),
            dma((halves,)),
            dma((halves,)),
            dma((n,)),
            dma((halves, n)),
            dma((halves * n,)),
            dma((halves,)),
            dma((halves,)),
            dma((halves, chips)),
            dma((halves, chips)),
            dma((chips,)),
            dma((chips,)),
        ],
        compiler_params=pltpu.CompilerParams(
            collective_id=0, has_side_effects=True, vmem_limit_bytes=56 * 1024 * 1024
        ),
        name="experts",
    )(
        tokens, upstream, expert_ids.T, gate_probs.T, pad_mask.reshape(1, tok),
        gate_weight, up_weight, down_weight,
    )
    return pl.pallas_call(
        copy_kernel, out_shape=result, in_specs=[local] * 2, out_specs=[local] * 2, name="results"
    )(*outs)


def shards(tokens, upstream, expert_ids, gate_probs, pad_mask, gate_weight, up_weight, down_weight):
    tok_count, top_count = expert_ids.shape
    experts = lax.axis_size("expert")
    capacity = min(tok_count, 2 * tok_count * top_count // experts)
    if capacity == tok_count and experts > 1 and experts & (experts - 1) == 0:
        return fused(
            tokens, upstream, expert_ids, gate_probs, pad_mask, gate_weight, up_weight, down_weight
        )
    slots_total = experts * capacity
    full_width = tokens.shape[1] * lax.axis_size("half")
    slot_dest = assign_slots(expert_ids, experts, capacity)
    place_items = placement_matrix(slot_dest, slots_total)
    place_tokens = jnp.sum(place_items.reshape(slots_total, tok_count, top_count), axis=2)
    weight_gate = gate_weight[0]
    weight_up = up_weight[0]
    weight_down = down_weight[0]
    rows_in = to_experts(place_tokens, tokens)
    gate_val = jnp.dot(rows_in, weight_gate, preferred_element_type=jnp.float32)
    up_val = jnp.dot(rows_in, weight_up, preferred_element_type=jnp.float32)
    hidden_act = (jax.nn.silu(gate_val) * up_val).astype(jnp.bfloat16)
    partial_value = jnp.dot(hidden_act, weight_down, preferred_element_type=jnp.float32)
    out_home = to_homes(partial_value)
    outputs = jnp.take(out_home, slot_dest, axis=0).reshape(tok_count, top_count, -1)
    out_float = outputs.astype(jnp.float32)
    shares = gate_probs / jnp.sum(gate_probs, axis=1, keepdims=True)
    layer_out = jnp.sum(shares[:, :, None] * out_float, axis=1).astype(jnp.bfloat16)
    gram_part = jnp.einsum("tjd,tkd->tjk", out_float, out_float) / math.sqrt(full_width)
    gram = lax.psum(gram_part, "half")
    off_diag = 1.0 - jnp.eye(top_count, dtype=jnp.float32)
    coeffs = orth_weight * gram * off_diag
    grad_out = pad_mask.astype(jnp.float32)[:, None, None] * (
        shares[:, :, None] * upstream.astype(jnp.float32)[:, None, :]
        + jnp.einsum("tjk,tkd->tjd", coeffs, out_float)
    )
    grad_items = grad_out.astype(jnp.bfloat16).reshape(tok_count * top_count, -1)
    grad_rows = to_experts(place_items, grad_items)
    grad_act = jnp.einsum("rd,hd->rh", grad_rows, weight_down, preferred_element_type=jnp.float32)
    sigma = jax.nn.sigmoid(gate_val)
    grad_gate = (grad_act * up_val * sigma * (1.0 + gate_val * (1.0 - sigma))).astype(jnp.bfloat16)
    grad_up = (grad_act * gate_val * sigma).astype(jnp.bfloat16)
    grad_partial = jnp.einsum(
        "rh,dh->rd", grad_gate, weight_gate, preferred_element_type=jnp.float32
    )
    grad_partial = grad_partial + jnp.einsum(
        "rh,dh->rd", grad_up, weight_up, preferred_element_type=jnp.float32
    )
    grad_home = to_homes(grad_partial)
    grad_pairs = jnp.take(grad_home, slot_dest, axis=0).reshape(tok_count, top_count, -1)
    grad_tokens = jnp.sum(grad_pairs.astype(jnp.float32), axis=1).astype(jnp.bfloat16)
    return (layer_out, grad_tokens)


def solution(mesh):
    in_specs = (
        P("expert", "half"),
        P("expert", "half"),
        P("expert", None),
        P("expert", None),
        P("expert"),
        P("expert", None, "half"),
        P("expert", None, "half"),
        P("expert", "half", None),
    )
    out_specs = (P("expert", "half"), P("expert", "half"))
    return jax.shard_map(shards, mesh=mesh, in_specs=in_specs, out_specs=out_specs, check_vma=False)
```
